32 devices in a mesh: section: 8 (over z, core), tensor: 4 (over y, x).
Axes of the slice: x: 2, y: 2, z: 4, core: 2. Of those that a mesh axis runs over, the one named last changes fastest.
Arguments:
- fwd_in: bfloat16 [8, 128, 2304], P('section', None, 'tensor'), may hold values from -6 to 6
- back_in: bfloat16 [8, 128, 2304], P('section', None, 'tensor'), may hold values from -0.59765625 to 0.59765625
- stash: bfloat16 [2, 8, 128, 2304], P(None, 'section', None, 'tensor'), may hold values from -6 to 6
- w_qkv: bfloat16 [8, 2304, 3, 4, 128], P('section', None, None, 'tensor'), may hold values from -0.125 to 0.125
- w_out: bfloat16 [8, 4, 128, 2304], P('section', 'tensor'), may hold values from -0.25 to 0.25
- norm_gain: bfloat16 [8, 2304], P('section'), may hold values from 0.25 to 1.75
- final_gain: bfloat16 [2304], replicated, may hold values from 0.25 to 1.75
- table: bfloat16 [8192, 2304], P(('section', 'tensor')), may hold values from -0.5625 to 0.5625
- ids: int32 [2, 128], replicated, may hold values from 0 to 8191
- back_ids: int32 [2, 128], replicated, may hold values from 0 to 8191
- targets: int32 [2, 128], replicated, may hold values from 0 to 8191
Outputs:
- fwd_out: bfloat16 [8, 128, 2304], P('section', None, 'tensor')
- back_out: bfloat16 [8, 128, 2304], P('section', None, 'tensor')
- table_grad: bfloat16 [8192, 2304], P(('section', 'tensor'))
- losses: float32 [2], replicated
The draws below stay inside these ranges and needn't reach their ends.
All inputs are finite; a program needn't handle non-finite values.
Results may differ from the reference program's by a relative error of at most 0.035.
Values may be sent and summed in bfloat16 or wider, within the bound.
No kernel may reach another device: no remote copies, remote signals or barrier semaphores. Data moves between devices by JAX's collectives and lax.ppermute only.
A program may use at most 64 MiB of HBM per device.

```python
import math
import jax
import jax.numpy as jnp
import numpy as np
from jax import lax

D = 2304
HEAD_DIM = 128
HEADS_DEV = 1
VOCAB_DEV = 256
ROWS = 128
TICKS = 2
SECTIONS = 8
HEADS = 4
VOCAB = 8192
N_SECTION = 8
N_TENSOR = 4
DEVICES = 32


def draw_table(key, part):
    rows = lax.iota(jnp.int32, VOCAB)
    column = rows // VOCAB_DEV % N_TENSOR
    frac = column.astype(jnp.float32) / float(max(N_TENSOR - 1, 1))
    base = jnp.clip(jax.random.normal(key, (VOCAB, D), jnp.float32), -6.0, 6.0)
    rise = jnp.exp(frac * math.log(3.0))
    return (base * rise[:, None] * (1.5 / math.sqrt(D))).astype(jnp.bfloat16)


def with_ends(result, stream_key, smallest, high):
    extent = result.shape
    spot = [jax.random.randint(jax.random.fold_in(stream_key, axis), (), 0, extent[axis]) for axis in range(len(extent))]
    result = result.at[tuple(spot)].set(smallest)
    longest = extent.index(max(extent))
    spot[longest] = (spot[longest] + 1) % extent[longest]
    return result.at[tuple(spot)].set(high)


def levels(key, shape, shards, least, largest):
    level = 1.0
    for dim, blocks in shards:
        steps = jax.random.uniform(jax.random.fold_in(jax.random.fold_in(key, 6), dim), (blocks,), jnp.float32, least / len(shards), largest / len(shards))
        level = level * jnp.repeat(jnp.exp(steps), shape[dim] // blocks).reshape((-1,) + (1,) * (len(shape) - 1 - dim))
    return level


def rank_bounds(amount, skew):
    portions = [(1 << 20) // math.isqrt(rank ** skew) + 1 for rank in range(1, amount + 1)]
    deviation = 1 + sum(portions) // (1 << 30)
    return np.cumsum(np.array([max(1, weight // deviation) for weight in portions]))


def ranked(key, extent, amount, lean):
    table = rank_bounds(amount, lean)
    lot = jax.random.randint(jax.random.fold_in(key, 1), extent, 0, int(table[amount - 1]))
    rank = jnp.searchsorted(jnp.asarray(table, jnp.int32), lot, side="right")
    return jax.random.permutation(jax.random.fold_in(key, 2), amount)[rank].astype(jnp.int32)


def bell_draw(rng, extent, deviation, bound, cuts=(), kind=jnp.bfloat16):
    result = deviation * jax.random.normal(rng, extent, jnp.float32)
    if cuts:
        result = result * levels(rng, extent, cuts, -0.22, 0.18)
    return jnp.clip(result, -bound, bound).astype(kind)


def setup_inputs(seed: int = 0) -> dict:
    splits = jax.random.split(jax.random.key(seed), 12)
    return {
        "fwd_in": bell_draw(splits[0], (SECTIONS, ROWS, D), 1.0, 6.0, ((0, 8), (2, 4))),
        "back_in": bell_draw(splits[1], (SECTIONS, ROWS, D), 0.1, 0.59765625, ((0, 8), (2, 4))),
        "stash": bell_draw(splits[2], (TICKS, SECTIONS, ROWS, D), 1.0, 6.0, ((1, 8), (3, 4))),
        "w_qkv": bell_draw(splits[3], (SECTIONS, D, 3, HEADS, HEAD_DIM), D ** -0.5, 0.125, ((0, 8), (3, 4))),
        "w_out": bell_draw(splits[4], (SECTIONS, HEADS, HEAD_DIM, D), (HEADS * HEAD_DIM) ** -0.5, 0.25, ((0, 8), (1, 4))),
        "norm_gain": jnp.clip(1.0 + 0.15 * jax.random.normal(splits[5], (SECTIONS, D), jnp.float32), 0.25, 1.75).astype(jnp.bfloat16),
        "final_gain": jnp.clip(1.0 + 0.15 * jax.random.normal(splits[6], (D,), jnp.float32), 0.25, 1.75).astype(jnp.bfloat16),
        "table": draw_table(jax.random.fold_in(splits[11], 71), 0),
        "ids": with_ends(jax.random.randint(splits[8], (TICKS, ROWS), 0, VOCAB), jax.random.fold_in(splits[8], 1), 0, VOCAB - 1).astype(jnp.int32),
        "back_ids": with_ends(ranked(splits[9], (TICKS, ROWS), VOCAB, 2), jax.random.fold_in(splits[9], 3), 0, VOCAB - 1).astype(jnp.int32),
        "targets": with_ends(ranked(splits[10], (TICKS, ROWS), VOCAB, 2), jax.random.fold_in(splits[10], 3), 0, VOCAB - 1).astype(jnp.int32),
    }


EPS = 1e-06
ATTN_CAP = 50.0
LOGIT_CAP = 30.0

def row_scale(values):
    return lax.rsqrt(lax.optimization_barrier(jnp.mean(values * values, axis=-1, keepdims=True)) + EPS)

def attend(normed, weights):
    qkv = jnp.einsum('rd,dchk->chrk', normed.astype(jnp.float32), weights.astype(jnp.float32)).astype(jnp.bfloat16)
    query, keys, values = (qkv[0], qkv[1], qkv[2])
    length = normed.shape[0]
    scores = jnp.einsum('hqk,hsk->hqs', query.astype(jnp.float32), keys.astype(jnp.float32)) * HEAD_DIM ** (-0.5)
    capped = jnp.tanh(scores / ATTN_CAP)
    places = lax.iota(jnp.int32, length)
    causal = places[None, :] <= places[:, None]
    raised = jnp.where(causal[None], jnp.exp(ATTN_CAP * capped), 0.0)
    probs = (raised / lax.optimization_barrier(jnp.sum(raised, axis=-1, keepdims=True))).astype(jnp.bfloat16)
    mixed = jnp.einsum('hqs,hsk->hqk', probs.astype(jnp.float32), values.astype(jnp.float32)).astype(jnp.bfloat16)
    return (query, keys, values, capped, probs, mixed)

def rounded_sum(parts):
    parts = lax.optimization_barrier(parts.astype(jnp.bfloat16)).astype(jnp.float32)
    return lax.optimization_barrier(jnp.sum(parts, axis=0))

def layer_forward(packed):
    acts, gain, weights, outw = packed
    xf = acts.astype(jnp.float32)
    scale = row_scale(xf)
    normed = (xf * scale * gain.astype(jnp.float32)).astype(jnp.bfloat16)
    mixed = attend(normed, weights)[5]
    length = acts.shape[0]
    groups = mixed.reshape(N_TENSOR, HEADS_DEV, length, HEAD_DIM).astype(jnp.float32)
    wgroups = outw.reshape(N_TENSOR, HEADS_DEV, HEAD_DIM, D).astype(jnp.float32)
    parts = jnp.einsum('ghrk,ghkd->grd', groups, wgroups)
    return (xf + rounded_sum(parts)).astype(jnp.bfloat16)

def layer_backward(packed):
    acts, upper, gain, weights, outw = packed
    xf = acts.astype(jnp.float32)
    gf = gain.astype(jnp.float32)
    scale = row_scale(xf)
    normed = (xf * scale * gf).astype(jnp.bfloat16)
    query, keys, values, capped, probs, mixed = attend(normed, weights)
    upperf = upper.astype(jnp.float32)
    dmix = jnp.einsum('rd,hkd->hrk', upperf, outw.astype(jnp.float32)).astype(jnp.bfloat16)
    dprob = jnp.einsum('hrk,hsk->hrs', dmix.astype(jnp.float32), values.astype(jnp.float32))
    pfull = probs.astype(jnp.float32)
    dscore = pfull * (dprob - lax.optimization_barrier(jnp.sum(dprob * pfull, axis=-1, keepdims=True)))
    dlogit = (dscore * (1.0 - capped * capped) * HEAD_DIM ** (-0.5)).astype(jnp.bfloat16)
    dlf = dlogit.astype(jnp.float32)
    dquery = jnp.einsum('hqs,hsk->hqk', dlf, keys.astype(jnp.float32)).astype(jnp.bfloat16)
    dkeys = jnp.einsum('hqs,hqk->hsk', dlf, query.astype(jnp.float32)).astype(jnp.bfloat16)
    dvalues = jnp.einsum('hqs,hqk->hsk', pfull, dmix.astype(jnp.float32)).astype(jnp.bfloat16)
    length = acts.shape[0]
    stacked = jnp.stack([dquery, dkeys, dvalues]).reshape(3, N_TENSOR, HEADS_DEV, length, HEAD_DIM).astype(jnp.float32)
    wgroups = weights.reshape(D, 3, N_TENSOR, HEADS_DEV, HEAD_DIM).astype(jnp.float32)
    parts = jnp.einsum('cghrk,dcghk->grd', stacked, wgroups)
    dnorm = rounded_sum(parts)
    dxf = scale * gf * dnorm - xf * scale ** 3 * lax.optimization_barrier(jnp.mean(xf * gf * dnorm, axis=-1, keepdims=True))
    return (upperf + dxf).astype(jnp.bfloat16)

def add_block(carry, pair):
    block_grad, block_rows = pair
    term = jnp.dot(block_grad, block_rows, preferred_element_type=jnp.float32)
    term = lax.optimization_barrier(term.astype(jnp.bfloat16)).astype(jnp.float32)
    return (carry + term, None)

def head(hidden, table, final_gain, target):
    xf = hidden.astype(jnp.float32)
    fg = final_gain.astype(jnp.float32)
    scale = row_scale(xf)
    normed = (xf * scale * fg).astype(jnp.bfloat16)
    raw = jnp.dot(normed, table.T, preferred_element_type=jnp.float32)
    capped = jnp.tanh(raw / LOGIT_CAP)
    logits = LOGIT_CAP * capped
    raised = jnp.exp(logits)
    total = lax.optimization_barrier(jnp.sum(raised, axis=-1))
    columns = lax.iota(jnp.int32, table.shape[0])
    hit = target[:, None] == columns[None, :]
    picked = lax.optimization_barrier(jnp.sum(jnp.where(hit, logits, 0.0), axis=-1))
    loss = jnp.mean(jnp.log(total) - picked)
    dlog = ((raised / total[:, None] - hit.astype(jnp.float32)) * (1.0 - capped * capped)).astype(jnp.bfloat16)
    length = hidden.shape[0]
    blocks = (jnp.transpose(dlog.reshape(length, DEVICES, VOCAB_DEV), (1, 0, 2)), table.reshape(DEVICES, VOCAB_DEV, D))
    dhid, unused = lax.scan(add_block, jnp.zeros((length, D), jnp.float32), blocks)
    head_grad = lax.dot_general(dlog, normed, (((0,), (0,)), ((), ())), preferred_element_type=jnp.float32)
    cot = scale * fg * dhid - xf * scale ** 3 * lax.optimization_barrier(jnp.mean(xf * fg * dhid, axis=-1, keepdims=True))
    return (loss, cot.astype(jnp.bfloat16), head_grad)

def reference(fwd_in, back_in, stash, w_qkv, w_out, norm_gain, final_gain, table, ids, back_ids, targets):
    emb_scale = math.sqrt(D)
    acts = fwd_in
    cots = back_in
    grad = jnp.zeros((VOCAB, D), jnp.float32)
    losses = []
    previous = acts[-1]
    for tick in range(TICKS):
        outs_fwd = lax.map(layer_forward, (acts, norm_gain, w_qkv, w_out))
        loss, cot_last, head_grad = head(outs_fwd[-1], table, final_gain, targets[tick])
        inputs_back = stash[tick]
        if tick > 0:
            inputs_back = inputs_back.at[N_SECTION - 1].set(previous)
        outs_back = lax.map(layer_backward, (inputs_back, cots, norm_gain, w_qkv, w_out))
        grad = grad + head_grad
        grad = grad.at[back_ids[tick]].add(outs_back[0].astype(jnp.float32) * emb_scale)
        first = (table[ids[tick]].astype(jnp.float32) * emb_scale).astype(jnp.bfloat16)
        previous = acts[-1]
        acts = jnp.concatenate([first[None], outs_fwd[:-1]], axis=0)
        cots = jnp.concatenate([outs_back[1:], cot_last[None]], axis=0)
        losses.append(loss)
    return (acts, cots, grad.astype(jnp.bfloat16), jnp.stack(losses))
```

```python
import math

import jax
import jax.numpy as jnp
from jax import lax
from jax.sharding import PartitionSpec as P

EPS = 1e-06
ATTN_CAP = 50.0
LOGIT_CAP = 30.0
F32 = jnp.float32
BF16 = jnp.bfloat16


def mm(a, b, ca, cb):
    return lax.dot_general(a, b, (((ca,), (cb,)), ((), ())), preferred_element_type=F32)


def row_scale(x):
    return lax.rsqrt(jnp.mean(x * x, axis=-1, keepdims=True) + EPS)


def gather(x, axis):
    return lax.all_gather(x, "tensor", axis=axis, tiled=True)


def exchange(x):
    return lax.all_to_all(x, "tensor", 0, 0, tiled=True)


def hop(x, pairs):
    return lax.ppermute(x, "section", pairs)


def from_section(x, root):
    sections = lax.axis_size("section")
    pos = lax.axis_index("section")
    core = root % 2
    got = jnp.where(pos == root, x, jnp.zeros_like(x))
    for chip in range(sections // 2):
        if chip != root // 2:
            got = got + hop(x, [(root, 2 * chip + core)])
    other = hop(got, [(2 * c + core, 2 * c + 1 - core) for c in range(sections // 2)])
    return jnp.where(pos % 2 == core, got, other)


def to_section(x, root):
    sections = lax.axis_size("section")
    core = root % 2
    pair = hop(x.astype(BF16), [(2 * c + 1 - core, 2 * c + core) for c in range(sections // 2)])
    total = x + pair.astype(F32)
    sent = total.astype(BF16)
    for chip in range(sections // 2):
        if chip != root // 2:
            total = total + hop(sent, [(2 * chip + core, root)]).astype(F32)
    return total


def sum_pieces(term, rows, width):
    t = lax.axis_size("tensor")
    parts = term.astype(BF16).reshape(rows, t, width)
    got = lax.all_to_all(parts, "tensor", 1, 1, tiled=True)
    return jnp.sum(got.astype(F32), axis=1)


def sum_all(x):
    x = jnp.sum(lax.all_gather(x, "tensor", axis=0), axis=0)
    sections = lax.axis_size("section")
    step = 1
    while step < sections:
        x = x + hop(x, [(i, i ^ step) for i in range(sections)])
        step *= 2
    return x


def attend(xfull, gain, wq):
    scale = row_scale(xfull)
    normed = (xfull * scale * gain).astype(BF16)
    width = wq.shape[1] // 3
    qkv = mm(normed, wq, 1, 0).astype(BF16)
    q, k, v = qkv[:, :width], qkv[:, width : 2 * width], qkv[:, 2 * width :]
    capped = jnp.tanh(mm(q, k, 1, 1) * width**-0.5 / ATTN_CAP)
    places = lax.iota(jnp.int32, q.shape[0])
    causal = places[None, :] <= places[:, None]
    raised = jnp.where(causal, jnp.exp(ATTN_CAP * capped), 0.0)
    probs = (raised / jnp.sum(raised, axis=-1, keepdims=True)).astype(BF16)
    return scale, qkv, capped, probs


def mixed(qkv, probs):
    width = qkv.shape[1] // 3
    return mm(probs, qkv[:, 2 * width :], 1, 0).astype(BF16)


def back_attend(saved, da, wq):
    scale, qkv, capped, probs = saved
    width = wq.shape[1] // 3
    q, k, v = qkv[:, :width], qkv[:, width : 2 * width], qkv[:, 2 * width :]
    dprob = mm(da, v, 1, 1)
    pfull = probs.astype(F32)
    dscore = pfull * (dprob - jnp.sum(dprob * pfull, axis=-1, keepdims=True))
    dlogit = (dscore * (1.0 - capped * capped) * width**-0.5).astype(BF16)
    dq = mm(dlogit, k, 1, 0).astype(BF16)
    dk = mm(dlogit, q, 0, 0).astype(BF16)
    dv = mm(probs, da, 0, 0).astype(BF16)
    dqkv = jnp.concatenate([dq, dk, dv], axis=1)
    stat = jnp.sum(dqkv.astype(F32) * qkv.astype(F32), axis=1)
    return mm(dqkv, wq, 1, 1), stat


def back_sum(term, stat, rows, width):
    t = lax.axis_size("tensor")
    high = stat.astype(BF16)
    low = (stat - high.astype(F32)).astype(BF16)
    extra = jnp.zeros((16, t, width), BF16)
    extra = extra.at[0, :, :rows].set(high[None]).at[1, :, :rows].set(low[None])
    parts = jnp.concatenate([term.astype(BF16).reshape(rows, t, width), extra], axis=0)
    got = lax.all_to_all(parts, "tensor", 1, 1, tiled=True)
    total = jnp.sum(got.astype(F32), axis=1)
    return total[:rows], total[rows, :rows] + total[rows + 1, :rows]


def body(
    fwd_in, back_in, stash, w_qkv, w_out, norm_gain, final_gain, table, ids, back_ids, targets
):
    pos = lax.axis_index("section")
    sections = lax.axis_size("section")
    tpos = lax.axis_index("tensor")
    tcount = lax.axis_size("tensor")
    acts = fwd_in[0]
    cots = back_in[0]
    rows, piece = acts.shape
    full = piece * tcount
    vocab = table.shape[0]
    first_col = (pos * tcount + tpos) * vocab
    columns = first_col + lax.iota(jnp.int32, vocab)
    emb_scale = math.sqrt(full)
    gain = norm_gain[0].astype(F32)
    gain_piece = lax.dynamic_slice_in_dim(gain, tpos * piece, piece, 0)
    fgain = final_gain.astype(F32)
    fgain_piece = lax.dynamic_slice_in_dim(fgain, tpos * piece, piece, 0)
    wq = w_qkv[0].reshape(full, -1)
    head = wq.shape[1] // 3
    outw = w_out[0].reshape(head, full)
    is_first = pos == 0
    is_last = pos == sections - 1
    ticks = ids.shape[0]

    xfull0 = gather(acts, 1)
    wo = lax.all_to_all(outw, "tensor", 1, 0, tiled=True)
    bfull = gather(stash[:, 0], 2)
    bfull1 = jnp.where(is_last, xfull0, bfull[1])

    def both(a, cot):
        part = mm(cot, wo, 1, 1).astype(BF16).reshape(rows, tcount, head)
        own = jnp.broadcast_to(a[:, None], (rows, tcount, head))
        got = lax.all_to_all(
            jnp.concatenate([own, part], axis=2), "tensor", 1, 1, tiled=True
        )
        a_all = got[:, :, :head].reshape(rows, tcount * head)
        return a_all, jnp.sum(got[:, :, head:].astype(F32), axis=1).astype(BF16)

    def only_da(cot):
        part = mm(cot, wo, 1, 1).astype(BF16).reshape(rows, tcount, head)
        got = lax.all_to_all(part, "tensor", 1, 1, tiled=True)
        return jnp.sum(got.astype(F32), axis=1).astype(BF16)

    def layer_out(x, a_all):
        return (x.astype(F32) + mm(a_all, wo, 1, 0)).astype(BF16)

    def back_out(saved, da, cot, xpiece):
        scale = saved[0]
        dnorm, stat = back_sum(*back_attend(saved, da, wq), rows, piece)
        xp = xpiece.astype(F32)
        out = (
            cot.astype(F32)
            + scale * gain_piece * dnorm
            - xp * (scale * scale * stat[:, None] / full)
        )
        return out.astype(BF16)

    saved_f0 = attend(xfull0.astype(F32), gain, wq)
    a0 = mixed(saved_f0[1], saved_f0[3])
    saved_b0 = attend(bfull[0].astype(F32), gain, wq)
    saved_b1 = attend(bfull1.astype(F32), gain, wq)

    a_all, da0 = both(a0, cots)
    y0 = layer_out(acts, a_all)
    gin0 = back_out(saved_b0, da0, cots, stash[0, 0])

    all_ids = ids.reshape(-1)
    hits = (all_ids[:, None] == columns[None, :]).astype(BF16)
    found = sum_pieces(mm(hits, table, 1, 0), ticks * rows, piece)
    entering = (to_section(found, 0) * emb_scale).astype(BF16)

    acts1 = jnp.where(
        is_first, entering[:rows], hop(y0, [(i, i + 1) for i in range(sections - 1)])
    )
    cots1 = hop(gin0, [(i + 1, i) for i in range(sections - 1)])
    xfull1 = gather(acts1, 1)
    saved_f1 = attend(xfull1.astype(F32), gain, wq)
    a1 = mixed(saved_f1[1], saved_f1[3])
    a_all1, da1 = both(a1, cots1)
    y1 = layer_out(acts1, a_all1)

    hpiece = from_section(jnp.concatenate([y0, y1], axis=0), sections - 1)
    hidden = gather(hpiece, 1).astype(F32)
    hscale = row_scale(hidden)
    hnormed = (hidden * hscale * fgain).astype(BF16)
    raw = mm(hnormed, table, 1, 1)
    capped = jnp.tanh(raw / LOGIT_CAP)
    raised = jnp.exp(LOGIT_CAP * capped)
    slope = 1.0 - capped * capped
    hit = targets.reshape(-1)[:, None] == columns[None, :]
    others = jnp.where(hit, 0.0, raised)
    sums = sum_all(
        jnp.stack(
            [
                jnp.sum(others, axis=1),
                jnp.sum(others * slope * raw, axis=1),
                jnp.sum(jnp.where(hit, raw, 0.0), axis=1),
            ]
        )
    )
    rest, weighted, raw_hit = sums[0], sums[1], sums[2]
    capped_hit = jnp.tanh(raw_hit / LOGIT_CAP)
    total = rest + jnp.exp(LOGIT_CAP * capped_hit)
    losses = jnp.mean(
        (jnp.log(total) - LOGIT_CAP * capped_hit).reshape(ticks, rows), axis=1
    )
    dlog = (jnp.where(hit, -rest[:, None], raised) / total[:, None] * slope).astype(BF16)
    hstat = (weighted - rest * (1.0 - capped_hit * capped_hit) * raw_hit) / total
    dhid = to_section(sum_pieces(mm(dlog, table, 1, 0), ticks * rows, piece), sections - 1)
    cot_last = (
        hscale * fgain_piece * dhid
        - hpiece.astype(F32) * (hscale * hscale * hstat[:, None] / full)
    ).astype(BF16)
    grad = mm(dlog, hnormed, 0, 0)

    cots1 = jnp.where(is_last, cot_last[:rows], cots1)
    da1 = jnp.where(is_last, only_da(cots1), da1)
    bpiece1 = jnp.where(is_last, acts, stash[1, 0])
    gin1 = back_out(saved_b1, da1, cots1, bpiece1)

    leaving = gather(from_section(jnp.concatenate([gin0, gin1], axis=0), 0), 1)
    back_hits = (back_ids.reshape(-1)[:, None] == columns[None, :]).astype(BF16)
    grad = grad + mm(back_hits, leaving, 0, 0) * emb_scale

    acts2 = jnp.where(
        is_first, entering[rows:], hop(y1, [(i, i + 1) for i in range(sections - 1)])
    )
    cots2 = jnp.where(
        is_last, cot_last[rows:], hop(gin1, [(i + 1, i) for i in range(sections - 1)])
    )
    return (acts2[None], cots2[None], grad.astype(BF16), losses)


def solution(mesh):
    return jax.shard_map(
        body,
        mesh=mesh,
        in_specs=(
            P("section", None, "tensor"),
            P("section", None, "tensor"),
            P(None, "section", None, "tensor"),
            P("section", None, None, "tensor", None),
            P("section", "tensor", None, None),
            P("section", None),
            P(),
            P(("section", "tensor"), None),
            P(),
            P(),
            P(),
        ),
        out_specs=(
            P("section", None, "tensor"),
            P("section", None, "tensor"),
            P(("section", "tensor"), None),
            P(),
        ),
        check_vma=False,
    )
```

```python
import functools
import math

import jax
import jax.numpy as jnp
from jax import lax
from jax.experimental import pallas as pl
from jax.experimental.pallas import tpu as pltpu
from jax.sharding import PartitionSpec as P

EPS = 1e-06
ATTN_CAP = 50.0
LOGIT_CAP = 30.0
F32 = jnp.float32
BF16 = jnp.bfloat16
EXTRA = 16


def dot(a, b, ca=1, cb=0):
    return lax.dot_general(a, b, (((ca,), (cb,)), ((), ())), preferred_element_type=F32)


def call(body, outs, args, name, flops=0, scratch=()):
    moved = sum(x.size * x.dtype.itemsize for x in args)
    moved += sum(math.prod(s) * jnp.dtype(d).itemsize for s, d in outs)
    vmem = pl.BlockSpec(memory_space=pltpu.VMEM)
    got = pl.pallas_call(
        body,
        out_shape=[jax.ShapeDtypeStruct(s, d) for s, d in outs],
        in_specs=[pl.BlockSpec(memory_space=pltpu.SMEM)] + [vmem] * (len(args) - 1),
        out_specs=[vmem] * len(outs),
        scratch_shapes=list(scratch),
        cost_estimate=pl.CostEstimate(flops=flops, bytes_accessed=moved, transcendentals=0),
        compiler_params=pltpu.CompilerParams(vmem_limit_bytes=24 << 20),
        name=name,
    )(*args)
    return got[0] if len(outs) == 1 else got


def block_of(here, d, size):
    return pl.ds(pl.multiple_of((here[0] ^ d) * size, size), size)


def rows_of(row, count):
    return jnp.broadcast_to(row, (count, row.shape[1]))


def split_rows(values):
    count = len(values)
    place = lax.broadcasted_iota(jnp.int32, (EXTRA, values[0].shape[1]), 0)
    out = jnp.zeros(place.shape, F32)
    for i, row in enumerate(values):
        high = row.astype(BF16).astype(F32)
        out = jnp.where(place == i, high, out)
        out = jnp.where(place == count + i, row - high, out)
    return out.astype(BF16)


def join_rows(extra, count):
    return [extra[i : i + 1, :] + extra[count + i : count + i + 1, :] for i in range(count)]


def tree_sum(parts):
    parts = list(parts)
    while len(parts) > 1:
        pairs = [parts[i] + parts[i + 1] for i in range(0, len(parts) - 1, 2)]
        parts = pairs + parts[len(parts) - len(parts) % 2 :]
    return parts[0]


def total_of(refs):
    return tree_sum([r[...].astype(F32) for r in refs])


def turn_column(row_ref, out_ref):
    full, width = out_ref.shape
    for at in range(0, full, width):
        part = jnp.broadcast_to(row_ref[0:1, at : at + width].astype(F32), (width, width))
        out_ref[at : at + width, :] = part.T.astype(BF16)


def prepare_kernel(n, here, x_ref, w_ref, gain_ref, fgain_ref, *refs):
    outs, (gcol_ref, fcol_ref, turned) = refs[:n], refs[n:]
    size = x_ref.shape[0]
    turned[...] = w_ref[...].T
    for d in range(n):
        outs[d][:size, :] = x_ref[...]
        outs[d][size:, :] = turned[block_of(here, d, size), :]
    turn_column(gain_ref, gcol_ref)
    turn_column(fgain_ref, fcol_ref)


def attend(x, gain, wq_ref):
    scale = lax.rsqrt(jnp.mean(x * x, axis=0, keepdims=True) + EPS)
    normed = (x * scale * gain).astype(BF16).T
    q = dot(normed, wq_ref[0]).astype(BF16)
    k = dot(normed, wq_ref[1]).astype(BF16)
    v = dot(normed, wq_ref[2]).astype(BF16)
    qt = q.T
    capped = jnp.tanh(dot(k, qt) * q.shape[1] ** -0.5 / ATTN_CAP)
    key = lax.broadcasted_iota(jnp.int32, capped.shape, 0)
    query = lax.broadcasted_iota(jnp.int32, capped.shape, 1)
    raised = jnp.where(key <= query, jnp.exp(ATTN_CAP * capped), 0.0)
    probs = (raised / jnp.sum(raised, axis=0, keepdims=True)).astype(BF16)
    return scale, qt, k, v, capped, probs


def forward_kernel(n, size, here, *refs):
    xs, (gain_ref, wq_ref, out, xfull) = refs[:n], refs[n:]
    for d in range(n):
        xfull[block_of(here, d, size), :] = xs[d][:size, :]
    x = xfull[...].astype(F32)
    _, _, _, v, _, probs = attend(x, gain_ref[...].astype(F32), wq_ref)
    out[...] = dot(v.T, probs).astype(BF16)


def forward_parts_kernel(n, size, here, *refs):
    xs, (gain_ref, wq_ref, cot_ref), outs, xfull = refs[:n], refs[n : n + 3], refs[n + 3 : -1], refs[-1]
    head = wq_ref.shape[-1]
    forward_kernel(n, size, here, *xs, gain_ref, wq_ref, outs[0].at[:head, :], xfull)
    for d in range(n):
        if d > 0:
            outs[d][:head, :] = outs[0][:head, :]
        part = dot(xs[d][size : 2 * size, :], cot_ref[...], 0, 0)
        outs[d][head:, :] = part.astype(BF16)


def recompute_kernel(n, tick, here, *refs):
    bs, refs = refs[:n], refs[n:]
    xs, refs = refs[: n * tick], refs[n * tick :]
    gain_ref, wq_ref, qkv_ref, v_ref, capped_ref, probs_ref, scale_ref, xfull = refs
    size = bs[0].shape[0]
    for d in range(n):
        block = bs[d][...]
        if tick > 0:
            block = jnp.where(here[2] == here[3] - 1, xs[d][:size, :], block)
        xfull[block_of(here, d, size), :] = block
    x = xfull[...].astype(F32)
    scale, qt, k, v, capped, probs = attend(x, gain_ref[...].astype(F32), wq_ref)
    qkv_ref[0] = qt
    qkv_ref[1] = k.T
    qkv_ref[2] = v.T
    v_ref[...] = v
    capped_ref[...] = capped
    probs_ref[...] = probs
    scale_ref[...] = rows_of(scale, 8)


def parts_kernel(n, size, here, cot_ref, *refs):
    wos, outs = refs[:n], refs[n:]
    for d in range(n):
        outs[d][...] = dot(wos[d][size : 2 * size, :], cot_ref[...], 0, 0).astype(BF16)


def layer_out_kernel(n, size, here, x_ref, first_ref, *refs):
    got, wos, (out, send_ref, own_ref) = refs[:n], refs[n : 2 * n], refs[2 * n :]
    head = wos[0].shape[1]
    total = x_ref[...].astype(F32)
    for d in range(n):
        total = total + dot(wos[d][size : 2 * size, :], got[d][:head, :])
    y = total.astype(BF16)
    out[...] = y
    send = jnp.where(here[2] % 2 == 0, first_ref[...], y)
    send_ref[...] = send
    own_ref[...] = jnp.where(here[2] >= here[3] - 2, send, jnp.zeros_like(send))


def back_kernel(n, here, *refs):
    got, refs = refs[:n], refs[n:]
    qkv_ref, v_ref, capped_ref, probs_ref, wq_ref = refs[:5]
    outs = refs[5:]
    head = v_ref.shape[1]
    first = got[0].shape[0] - head
    da = sum(g[first:, :].astype(F32) for g in got).astype(BF16)
    probs = probs_ref[...]
    pfull = probs.astype(F32)
    dprob = dot(v_ref[...], da)
    dscore = pfull * (dprob - jnp.sum(dprob * pfull, axis=0, keepdims=True))
    capped = capped_ref[...]
    dlogit = (dscore * (1.0 - capped * capped) * head**-0.5).astype(BF16)
    grads = (
        dot(qkv_ref[1], dlogit).astype(BF16),
        dot(qkv_ref[0], dlogit, 1, 1).astype(BF16),
        dot(da, probs, 1, 1).astype(BF16),
    )
    stat = sum(
        jnp.sum(g.astype(F32) * qkv_ref[i].astype(F32), axis=0, keepdims=True)
        for i, g in enumerate(grads)
    )
    stat = split_rows([stat])
    size = outs[0].shape[0] - EXTRA
    for d in range(n):
        at = block_of(here, d, size)
        term = sum(dot(wq_ref[i, at, :], g) for i, g in enumerate(grads))
        outs[d][:size, :] = term.astype(BF16)
        outs[d][size:, :] = stat


def back_out_kernel(n, full, lasts, here, *refs):
    got, refs = refs[:n], refs[n:]
    scale_ref, gain_ref, x_ref, last_x_ref, cot_ref, other_ref, out = refs
    size = x_ref.shape[0]
    total = total_of(got)
    (stat,) = join_rows(total[size:, :], 1)
    scale = scale_ref[0:1, :]
    gain = gain_ref[block_of(here, 0, size), :].astype(F32)
    x = jnp.where(here[2] == here[3] - 1, last_x_ref[...], x_ref[...]).astype(F32)
    dx = (
        cot_ref[...].astype(F32)
        + scale * gain * total[:size, :]
        - x * (scale * scale * stat / full)
    )
    out[...] = jnp.where(here[2] >= here[3] - lasts, dx.astype(BF16), other_ref[...])


def lookup_kernel(here, ids_ref, targets_ref, table_ref, turned_ref, *outs):
    turned_ref[...] = table_ref[...].T
    vocab = turned_ref.shape[1]
    ticks, rows = ids_ref.shape
    column = here[1] + lax.broadcasted_iota(jnp.int32, (vocab, rows), 0)
    even = here[2] % 2 == 0
    for t in range(ticks):
        ids, targets = ids_ref[t : t + 1, :], targets_ref[t : t + 1, :]
        wanted = (jnp.where(even, ids, targets), jnp.where(even, targets, ids))
        for out, row in zip(outs, wanted):
            hits = (column == row).astype(F32).astype(BF16)
            out[:, t * rows : (t + 1) * rows] = dot(turned_ref[...], hits).astype(BF16)


def pair_kernel(here, keep_ref, got_ref, *outs):
    size = outs[0].shape[0]
    for d, out in enumerate(outs):
        at = block_of(here, d, size)
        out[...] = (keep_ref[at, :].astype(F32) + got_ref[at, :].astype(F32)).astype(BF16)


def assemble_kernel(n, here, *refs):
    parts, out = refs[:n], refs[n]
    for d in range(n):
        out[block_of(here, d, parts[d].shape[0]), :] = parts[d][...]


def pick_kernel(here, even_ref, odd_ref, send_ref, own_ref):
    send = jnp.where(here[2] % 2 == 0, even_ref[...], odd_ref[...])
    send_ref[...] = send
    own_ref[...] = jnp.where(here[2] < 2, send, jnp.zeros_like(send))


def enter_kernel(tick, emb_scale, here, y_ref, *refs):
    found, out = refs[:-1], refs[-1]
    rows = y_ref.shape[1]
    entering = tree_sum([f[:, tick * rows : (tick + 1) * rows].astype(F32) for f in found])
    entering = (entering * emb_scale).astype(BF16)
    out[...] = jnp.where(here[2] == 0, entering, y_ref[...])


def head_kernel(n, flip, here, h_ref, gain_ref, table_ref, turned_ref, target_ref, *refs):
    normed_ref, raw_ref, scale_ref, out = refs
    size = out.shape[0] // n - EXTRA
    h = h_ref[...].astype(F32)
    scale = lax.rsqrt(jnp.mean(h * h, axis=0, keepdims=True) + EPS)
    normed = (h * scale * gain_ref[...].astype(F32)).astype(BF16)
    normed_ref[...] = normed
    raw = dot(table_ref[...], normed)
    raw_ref[...] = raw
    scale_ref[...] = rows_of(scale, 8)
    column = here[1] + lax.broadcasted_iota(jnp.int32, raw.shape, 0)
    target = jnp.where(here[2] % 2 == flip, target_ref[0:1, :], target_ref[1:2, :])
    hit = column == target
    capped = jnp.tanh(raw / LOGIT_CAP)
    others = jnp.where(hit, 0.0, jnp.exp(LOGIT_CAP * capped))
    weighted = others * (1.0 - capped * capped)
    extra = split_rows(
        [
            jnp.sum(others, axis=0, keepdims=True),
            jnp.sum(weighted * raw, axis=0, keepdims=True),
            jnp.sum(jnp.where(hit, raw, 0.0), axis=0, keepdims=True),
        ]
    )
    weighted = weighted.astype(BF16)
    for d in range(n):
        at = d * (size + EXTRA)
        term = dot(turned_ref[block_of(here, d, size), :], weighted)
        out[at : at + size, :] = term.astype(BF16)
        out[at + size : at + size + EXTRA, :] = extra


def add_terms(total, out):
    size = out.shape[0] - EXTRA
    out[:size, :] = total[:size, :].astype(BF16)
    out[size:, :] = split_rows(join_rows(total[size:, :], 3))


def pair_terms_kernel(here, keep_ref, got_ref, *outs):
    step = outs[0].shape[0]
    for d, out in enumerate(outs):
        cut = slice(d * step, (d + 1) * step)
        add_terms(keep_ref[cut, :].astype(F32) + got_ref[cut, :].astype(F32), out)


def sum_kernel(here, *refs):
    add_terms(total_of(refs[:-1]), refs[-1])


def cot_kernel(tick, full, here, total_ref, scale_ref, h_ref, gain_ref, *refs):
    found, (out, sums_ref) = refs[:-2], refs[-2:]
    size, rows = h_ref.shape
    gain = gain_ref[block_of(here, 0, size), :].astype(F32)
    rest, weighted, raw_hit = join_rows(total_ref[size:, :].astype(F32), 3)
    capped = jnp.tanh(raw_hit / LOGIT_CAP)
    slope = 1.0 - capped * capped
    whole = rest + jnp.exp(LOGIT_CAP * capped)
    target = tree_sum([f[:, tick * rows : (tick + 1) * rows].astype(F32) for f in found])
    dhid = (total_ref[:size, :].astype(F32) - target * (rest * slope)) / whole
    stat = (weighted - rest * slope * raw_hit) / whole
    scale = scale_ref[0:1, :]
    out[...] = (
        scale * gain * dhid - h_ref[...].astype(F32) * (scale * scale * stat / full)
    ).astype(BF16)
    place = lax.broadcasted_iota(jnp.int32, (8, rows), 0)
    sums = jnp.where(place == 0, rest, jnp.where(place == 1, raw_hit, 0.0))
    sums_ref[...] = jnp.where(here[2] == here[3] - 1, sums, 0.0)


def grad_kernel(ticks, emb_scale, here, ids_ref, targets_ref, sums_ref, *refs):
    out, loss_ref = refs[-2:]
    vocab, rows = refs[0].shape
    column = here[1] + lax.broadcasted_iota(jnp.int32, (vocab, rows), 0)
    place = lax.broadcasted_iota(jnp.int32, loss_ref.shape, 0)
    losses = jnp.zeros(loss_ref.shape, F32)
    for t in range(ticks):
        rest, raw_hit = sums_ref[8 * t : 8 * t + 1, :], sums_ref[8 * t + 1 : 8 * t + 2, :]
        logit = LOGIT_CAP * jnp.tanh(raw_hit / LOGIT_CAP)
        loss = jnp.mean(jnp.log(rest + jnp.exp(logit)) - logit, axis=1, keepdims=True)
        losses = jnp.where(place == t, jnp.broadcast_to(loss, losses.shape), losses)
    loss_ref[...] = losses
    dlogs, hits = [], []
    for flip in range(2):
        first = here[2] % 2 == flip
        sums = jnp.where(first, sums_ref[0:8, :], sums_ref[8:16, :])
        rest, raw_hit = sums[0:1, :], sums[1:2, :]
        whole = rest + jnp.exp(LOGIT_CAP * jnp.tanh(raw_hit / LOGIT_CAP))
        capped = jnp.tanh(refs[3 * flip][...] / LOGIT_CAP)
        hit = column == jnp.where(first, targets_ref[0:1, :], targets_ref[1:2, :])
        top = jnp.where(hit, -rest, jnp.exp(LOGIT_CAP * capped))
        dlogs.append((top / whole * (1.0 - capped * capped)).astype(BF16))
        hit = column == jnp.where(first, ids_ref[0:1, :], ids_ref[1:2, :])
        hits.append(hit.astype(F32).astype(BF16))
    full = out.shape[1]
    step = 256 if full % 256 == 0 else full
    for at in range(0, full, step):
        cut = slice(at, at + step)
        looked = sum(dot(hits[i], refs[3 * i + 2][cut, :], 1, 1) for i in range(2))
        heads = sum(dot(dlogs[i], refs[3 * i + 1][cut, :], 1, 1) for i in range(2))
        out[:, cut] = (heads + looked * emb_scale).astype(BF16)


def last_cots_kernel(here, gin_ref, cot_ref, out):
    out[...] = jnp.where(here[2] == here[3] - 1, cot_ref[...], gin_ref[...])


def after(x, *others):
    return lax.optimization_barrier((x, *others))[0]


def hop(x, pairs):
    return lax.ppermute(x, "section", pairs)


def swap(blocks, sections=None):
    n = lax.axis_size("tensor")
    if sections is None:
        return [blocks[0]] + [
            lax.ppermute(blocks[d], "tensor", [(i, i ^ d) for i in range(n)])
            for d in range(1, n)
        ]
    out = [blocks[0]]
    for d in range(1, n):
        pairs = [(s * n + i, s * n + (i ^ d)) for s in sections for i in range(n)]
        out.append(lax.ppermute(blocks[d], ("section", "tensor"), pairs))
    return out


def share(x):
    return swap([x] * lax.axis_size("tensor"))


def other_chips(root):
    core = root % 2
    return [
        2 * c + core for c in range(lax.axis_size("section") // 2) if c != root // 2
    ]


def along_chips(x, root):
    return [hop(x, [(root, s)]) for s in other_chips(root)]


def across(root):
    return [(s, s ^ 1) for s in [root] + other_chips(root)]


def from_chip(own, send, root):
    for s in other_chips(root):
        own = own + hop(send, [(root, s), (root ^ 1, s ^ 1)])
    return own


def to_chips(x, even_root, odd_root):
    sources = zip(other_chips(even_root), other_chips(odd_root))
    return [x] + [hop(x, [(a, even_root), (b, odd_root)]) for a, b in sources]


def other_core(x):
    return hop(x, [(i, i ^ 1) for i in range(lax.axis_size("section"))])


def body(
    fwd_in, back_in, stash, w_qkv, w_out, norm_gain, final_gain, table, ids, back_ids, targets
):
    pos = lax.axis_index("section")
    sections = lax.axis_size("section")
    tpos = lax.axis_index("tensor")
    n = lax.axis_size("tensor")
    rows, piece = fwd_in.shape[1:]
    full = piece * n
    vocab = table.shape[0]
    ticks = ids.shape[0]
    head = w_qkv.shape[-1]
    last = sections - 1
    emb_scale = math.sqrt(full)
    here = jnp.stack([tpos, (pos * n + tpos) * vocab, pos, jnp.full_like(pos, sections)])
    here = here.astype(jnp.int32)
    up = [(i, i + 1) for i in range(last)]
    down = [(i + 1, i) for i in range(last)]

    acts = fwd_in[0].T
    cots = back_in[0].T
    held0, held1 = stash[0, 0].T, stash[1, 0].T
    wq = w_qkv[0, :, :, 0, :].transpose(1, 0, 2)

    work = (2 * full * rows * 3 * head) + 4 * rows * rows * head
    act = ((piece, rows), BF16)
    wide = ((full, rows), BF16)
    message = ((piece + EXTRA, rows), BF16)
    whole_x = [pltpu.VMEM((full, rows), BF16)]

    *first, gain, fgain = call(
        functools.partial(prepare_kernel, n),
        [((2 * piece, rows), BF16)] * n + [wide] * 2,
        [here, acts, w_out[0, 0], norm_gain, final_gain[None]],
        "prepare",
        scratch=[pltpu.VMEM((full, head), BF16)],
    )
    base = swap(first)
    turned, *rows_found = call(
        lookup_kernel,
        [((full, vocab), BF16)] + [((full, ticks * rows), BF16)] * 2,
        [here, ids, targets, after(table, gain)],
        "lookup",
        4 * full * rows * vocab * ticks,
    )

    def look_up(keep, send):
        found = call(
            pair_kernel,
            [((piece, ticks * rows), BF16)] * n,
            [here, keep, other_core(send)],
            "pair",
        )
        return tree_sum([b.astype(F32) for b in swap(found)]).astype(BF16)

    found = look_up(*rows_found)

    def layer_out(x, got, earlier):
        return call(
            functools.partial(layer_out_kernel, n, piece),
            [act] * 3,
            [here, x, earlier, *got, *base],
            "layer_out",
            2 * piece * rows * head * n,
        )

    def back(got, saved):
        return call(
            functools.partial(back_kernel, n),
            [message] * n,
            [here, *got, *saved[:4], wq],
            "back",
            work,
        )

    def back_out(got, saved, x, last_x, cot, other=None):
        return call(
            functools.partial(back_out_kernel, n, full, sections if other is None else 1),
            [act],
            [here, *got, saved[4], gain, x, last_x, cot, cot if other is None else other],
            "back_out",
        )

    def parts(cot):
        return call(
            functools.partial(parts_kernel, n, piece),
            [((head, rows), BF16)] * n,
            [here, cot, *base],
            "parts",
        )

    def assemble(parts):
        return call(functools.partial(assemble_kernel, n), [wide], [here, *parts], "assemble")

    def run_head(h, flip):
        return call(
            functools.partial(head_kernel, n, flip),
            [wide, ((vocab, rows), F32), ((8, rows), F32), ((n * message[0][0], rows), BF16)],
            [here, h, fgain, table, turned, targets],
            "head",
            4 * full * rows * vocab,
        )

    def recompute(bs, tick):
        return call(
            functools.partial(recompute_kernel, n, tick),
            [
                ((3, head, rows), BF16),
                ((rows, head), BF16),
                ((rows, rows), F32),
                ((rows, rows), BF16),
                ((8, rows), F32),
            ],
            [here, *bs, *(base if tick > 0 else []), gain, wq],
            "recompute",
            work,
            whole_x,
        )

    messages = call(
        functools.partial(forward_parts_kernel, n, piece),
        [((2 * head, rows), BF16)] * n,
        [here, *after(base, found), gain, wq, cots],
        "forward",
        work,
        whole_x,
    )
    looked = to_chips(found, 0, last)
    got0 = swap(messages)
    y0, _, _ = layer_out(acts, got0, acts)
    y0_even = hop(y0, [(last, last - 1)])
    saved0 = recompute(share(after(held0, y0)), 0)
    terms0 = back(got0, saved0)

    acts1 = call(
        functools.partial(enter_kernel, 0, emb_scale),
        [act],
        [here, hop(y0, up), *looked],
        "enter",
    )
    a1 = call(
        functools.partial(forward_kernel, n, piece),
        [((head, rows), BF16)],
        [here, *after(share(acts1), terms0[0]), gain, wq],
        "forward",
        work,
        whole_x,
    )
    y1, h_send, h_own = layer_out(acts1, share(a1), y0_even)

    gin0 = back_out(swap(after(terms0, y1)), saved0, held0, held0, cots)
    saved1 = recompute(share(after(held1, y1)), 1)
    cots1 = hop(gin0, down)
    h_mine = after(from_chip(h_own, h_send, last), gin0, saved1[1])
    h_mine = assemble(share(h_mine))
    h_other = other_core(h_mine)

    normed_a, raw_a, scale_a, terms_a = run_head(h_mine, 0)
    normed_b, raw_b, scale_b, terms_b = run_head(h_other, 1)
    y1_up = hop(after(y1, h_mine), up)
    parts1 = swap(parts(after(cots1, raw_b)))
    acts2 = call(
        functools.partial(enter_kernel, 1, emb_scale),
        [act],
        [here, y1_up, *looked],
        "enter",
    )
    terms = call(
        pair_terms_kernel,
        [message] * n,
        [here, after(terms_a, acts2), other_core(terms_b)],
        "pair_terms",
    )
    gin1 = back_out(
        swap(back(after(parts1, terms), saved1)), saved1, held1, acts, cots1
    )
    total = call(sum_kernel, [message], [here, *swap(terms)], "sum")
    g_send, g_own = call(pick_kernel, [act] * 2, [here, gin0, hop(gin1, [(0, 1)])], "pick")
    total = to_chips(total, last - 1, last)
    total = call(sum_kernel, [message], [here, *after(total, g_own)], "sum")

    def cot_of(tick, total, scale, h):
        return call(
            functools.partial(cot_kernel, tick, full),
            [act, ((8, rows), F32)],
            [here, total, scale, h, fgain, *looked],
            "cot",
        )

    cot0, sums0 = cot_of(0, hop(total, [(last - 1, last)]), scale_b, y0)

    late_parts = parts(cot0)
    late_terms = back(swap(late_parts, [last]), saved1)
    leaving_a = assemble(share(after(from_chip(g_own, g_send, 0), late_parts[0])))
    leaving_b = other_core(leaving_a)
    cot1, sums1 = cot_of(1, after(total, late_parts[0]), scale_a, y1)
    sums = jnp.concatenate([sums0, sums1], axis=0)
    for part in along_chips(sums, last):
        sums = sums + part
    late_terms = after(swap(late_terms, [last]), leaving_a, sums)
    late = back_out(late_terms, saved1, held1, acts, cot0, gin1)
    late_down = hop(late, down)
    sums = after(sums, late)
    sums = sums + hop(sums, across(last))
    grad, losses = call(
        functools.partial(grad_kernel, ticks, emb_scale),
        [((vocab, full), BF16), ((8, rows), F32)],
        [
            *(here, back_ids, targets, sums),
            *(raw_a, normed_a, leaving_a),
            *(raw_b, normed_b, leaving_b),
        ],
        "grad",
        8 * full * rows * vocab,
    )
    cots2 = call(last_cots_kernel, [act], [here, late_down, cot1], "last_cots")
    return (acts2.T[None], cots2.T[None], grad, losses[:ticks, 0])


def solution(mesh):
    return jax.shard_map(
        body,
        mesh=mesh,
        in_specs=(
            P("section", None, "tensor"),
            P("section", None, "tensor"),
            P(None, "section", None, "tensor"),
            P("section", None, None, "tensor", None),
            P("section", "tensor", None, None),
            P("section", None),
            P(),
            P(("section", "tensor"), None),
            P(),
            P(),
            P(),
        ),
        out_specs=(
            P("section", None, "tensor"),
            P("section", None, "tensor"),
            P(("section", "tensor"), None),
            P(),
        ),
        check_vma=False,
    )
```

```python
import functools
import math

import jax
import jax.numpy as jnp
from jax import lax
from jax.experimental import pallas as pl
from jax.experimental.pallas import tpu as pltpu
from jax.sharding import PartitionSpec as P

EPS = 1e-06
ATTN_CAP = 50.0
LOGIT_CAP = 30.0
F32 = jnp.float32
BF16 = jnp.bfloat16
EXTRA = 16


def dot(a, b, ca=1, cb=0):
    return lax.dot_general(a, b, (((ca,), (cb,)), ((), ())), preferred_element_type=F32)


def call(body, outs, args, name, flops=0, scratch=()):
    moved = sum(x.size * x.dtype.itemsize for x in args)
    moved += sum(math.prod(s) * jnp.dtype(d).itemsize for s, d in outs)
    vmem = pl.BlockSpec(memory_space=pltpu.VMEM)
    got = pl.pallas_call(
        body,
        out_shape=[jax.ShapeDtypeStruct(s, d) for s, d in outs],
        in_specs=[pl.BlockSpec(memory_space=pltpu.SMEM)] + [vmem] * (len(args) - 1),
        out_specs=[vmem] * len(outs),
        scratch_shapes=list(scratch),
        cost_estimate=pl.CostEstimate(flops=flops, bytes_accessed=moved, transcendentals=0),
        compiler_params=pltpu.CompilerParams(vmem_limit_bytes=24 << 20),
        name=name,
    )(*args)
    return got[0] if len(outs) == 1 else got


def block_of(here, d, size):
    return pl.ds(pl.multiple_of((here[0] ^ d) * size, size), size)


def rows_of(row, count):
    return jnp.broadcast_to(row, (count, row.shape[1]))


def split_rows(values):
    count = len(values)
    place = lax.broadcasted_iota(jnp.int32, (EXTRA, values[0].shape[1]), 0)
    out = jnp.zeros(place.shape, F32)
    for i, row in enumerate(values):
        high = row.astype(BF16).astype(F32)
        out = jnp.where(place == i, high, out)
        out = jnp.where(place == count + i, row - high, out)
    return out.astype(BF16)


def join_rows(extra, count):
    return [extra[i : i + 1, :] + extra[count + i : count + i + 1, :] for i in range(count)]


def tree_sum(parts):
    parts = list(parts)
    while len(parts) > 1:
        pairs = [parts[i] + parts[i + 1] for i in range(0, len(parts) - 1, 2)]
        parts = pairs + parts[len(parts) - len(parts) % 2 :]
    return parts[0]


def total_of(refs):
    return tree_sum([r[...].astype(F32) for r in refs])


def turn_column(row_ref, out_ref):
    full, width = out_ref.shape
    for at in range(0, full, width):
        part = jnp.broadcast_to(row_ref[0:1, at : at + width].astype(F32), (width, width))
        out_ref[at : at + width, :] = part.T.astype(BF16)


def prepare_kernel(n, here, x_ref, w_ref, gain_ref, fgain_ref, *refs):
    outs, (gcol_ref, fcol_ref, turned) = refs[:n], refs[n:]
    size = x_ref.shape[0]
    turned[...] = w_ref[...].T
    for d in range(n):
        outs[d][:size, :] = x_ref[...]
        outs[d][size:, :] = turned[block_of(here, d, size), :]
    turn_column(gain_ref, gcol_ref)
    turn_column(fgain_ref, fcol_ref)


def attend(x, gain, wq_ref):
    scale = lax.rsqrt(jnp.mean(x * x, axis=0, keepdims=True) + EPS)
    normed = (x * scale * gain).astype(BF16).T
    q = dot(normed, wq_ref[0]).astype(BF16)
    k = dot(normed, wq_ref[1]).astype(BF16)
    v = dot(normed, wq_ref[2]).astype(BF16)
    qt = q.T
    capped = jnp.tanh(dot(k, qt) * q.shape[1] ** -0.5 / ATTN_CAP)
    key = lax.broadcasted_iota(jnp.int32, capped.shape, 0)
    query = lax.broadcasted_iota(jnp.int32, capped.shape, 1)
    raised = jnp.where(key <= query, jnp.exp(ATTN_CAP * capped), 0.0)
    probs = (raised / jnp.sum(raised, axis=0, keepdims=True)).astype(BF16)
    return scale, qt, k, v, capped, probs


def forward_kernel(n, size, here, *refs):
    xs, (gain_ref, wq_ref, out, xfull) = refs[:n], refs[n:]
    for d in range(n):
        xfull[block_of(here, d, size), :] = xs[d][:size, :]
    x = xfull[...].astype(F32)
    _, _, _, v, _, probs = attend(x, gain_ref[...].astype(F32), wq_ref)
    out[...] = dot(v.T, probs).astype(BF16)


def forward_parts_kernel(n, size, here, *refs):
    xs, (gain_ref, wq_ref, cot_ref), outs, xfull = refs[:n], refs[n : n + 3], refs[n + 3 : -1], refs[-1]
    head = wq_ref.shape[-1]
    forward_kernel(n, size, here, *xs, gain_ref, wq_ref, outs[0].at[:head, :], xfull)
    for d in range(n):
        if d > 0:
            outs[d][:head, :] = outs[0][:head, :]
        part = dot(xs[d][size : 2 * size, :], cot_ref[...], 0, 0)
        outs[d][head:, :] = part.astype(BF16)


def recompute_kernel(n, tick, here, *refs):
    bs, refs = refs[:n], refs[n:]
    xs, refs = refs[: n * tick], refs[n * tick :]
    gain_ref, wq_ref, qkv_ref, v_ref, capped_ref, probs_ref, scale_ref, xfull = refs
    size = bs[0].shape[0]
    for d in range(n):
        block = bs[d][...]
        if tick > 0:
            block = jnp.where(here[2] == here[3] - 1, xs[d][:size, :], block)
        xfull[block_of(here, d, size), :] = block
    x = xfull[...].astype(F32)
    scale, qt, k, v, capped, probs = attend(x, gain_ref[...].astype(F32), wq_ref)
    qkv_ref[0] = qt
    qkv_ref[1] = k.T
    qkv_ref[2] = v.T
    v_ref[...] = v
    capped_ref[...] = capped
    probs_ref[...] = probs
    scale_ref[...] = rows_of(scale, 8)


def parts_kernel(n, size, here, cot_ref, last_cot_ref, *refs):
    wos, outs = refs[:n], refs[n:]
    cot = jnp.where(here[2] == here[3] - 1, last_cot_ref[...], cot_ref[...])
    for d in range(n):
        outs[d][...] = dot(wos[d][size : 2 * size, :], cot, 0, 0).astype(BF16)


def layer_out_kernel(n, size, here, x_ref, first_ref, *refs):
    got, wos, (out, send_ref, own_ref) = refs[:n], refs[n : 2 * n], refs[2 * n :]
    head = wos[0].shape[1]
    total = x_ref[...].astype(F32)
    for d in range(n):
        total = total + dot(wos[d][size : 2 * size, :], got[d][:head, :])
    y = total.astype(BF16)
    out[...] = y
    send = jnp.where(here[2] % 2 == 0, first_ref[...], y)
    send_ref[...] = send
    own_ref[...] = jnp.where(here[2] >= here[3] - 2, send, jnp.zeros_like(send))


def back_kernel(n, here, *refs):
    got, refs = refs[:n], refs[n:]
    qkv_ref, v_ref, capped_ref, probs_ref, wq_ref = refs[:5]
    outs = refs[5:]
    head = v_ref.shape[1]
    first = got[0].shape[0] - head
    da = sum(g[first:, :].astype(F32) for g in got).astype(BF16)
    probs = probs_ref[...]
    pfull = probs.astype(F32)
    dprob = dot(v_ref[...], da)
    dscore = pfull * (dprob - jnp.sum(dprob * pfull, axis=0, keepdims=True))
    capped = capped_ref[...]
    dlogit = (dscore * (1.0 - capped * capped) * head**-0.5).astype(BF16)
    grads = (
        dot(qkv_ref[1], dlogit).astype(BF16),
        dot(qkv_ref[0], dlogit, 1, 1).astype(BF16),
        dot(da, probs, 1, 1).astype(BF16),
    )
    stat = sum(
        jnp.sum(g.astype(F32) * qkv_ref[i].astype(F32), axis=0, keepdims=True)
        for i, g in enumerate(grads)
    )
    stat = split_rows([stat])
    size = outs[0].shape[0] - EXTRA
    for d in range(n):
        at = block_of(here, d, size)
        term = sum(dot(wq_ref[i, at, :], g) for i, g in enumerate(grads))
        outs[d][:size, :] = term.astype(BF16)
        outs[d][size:, :] = stat


def back_out_kernel(n, full, here, *refs):
    got, refs = refs[:n], refs[n:]
    scale_ref, gain_ref, x_ref, last_x_ref, cot_ref, last_cot_ref, out = refs
    size = x_ref.shape[0]
    total = total_of(got)
    (stat,) = join_rows(total[size:, :], 1)
    scale = scale_ref[0:1, :]
    gain = gain_ref[block_of(here, 0, size), :].astype(F32)
    is_last = here[2] == here[3] - 1
    x = jnp.where(is_last, last_x_ref[...], x_ref[...]).astype(F32)
    cot = jnp.where(is_last, last_cot_ref[...], cot_ref[...]).astype(F32)
    out[...] = (
        cot
        + scale * gain * total[:size, :]
        - x * (scale * scale * stat / full)
    ).astype(BF16)


def lookup_kernel(here, ids_ref, targets_ref, table_ref, turned_ref, *outs):
    turned_ref[...] = table_ref[...].T
    vocab = turned_ref.shape[1]
    ticks, rows = ids_ref.shape
    column = here[1] + lax.broadcasted_iota(jnp.int32, (vocab, rows), 0)
    even = here[2] % 2 == 0
    for t in range(ticks):
        ids, targets = ids_ref[t : t + 1, :], targets_ref[t : t + 1, :]
        wanted = (jnp.where(even, ids, targets), jnp.where(even, targets, ids))
        for out, row in zip(outs, wanted):
            hits = (column == row).astype(F32).astype(BF16)
            out[:, t * rows : (t + 1) * rows] = dot(turned_ref[...], hits).astype(BF16)


def pair_kernel(n, here, keep_ref, got_ref, *outs):
    size, rows = outs[0].shape
    for i, out in enumerate(outs):
        at, t = block_of(here, i % n, size), i // n
        cut = slice(t * rows, (t + 1) * rows)
        out[...] = (keep_ref[at, cut].astype(F32) + got_ref[at, cut].astype(F32)).astype(BF16)


def assemble_kernel(n, here, *refs):
    parts, out = refs[:n], refs[n]
    for d in range(n):
        out[block_of(here, d, parts[d].shape[0]), :] = parts[d][...]


def pick_kernel(here, even_ref, odd_ref, send_ref, own_ref):
    send = jnp.where(here[2] % 2 == 0, even_ref[...], odd_ref[...])
    send_ref[...] = send
    own_ref[...] = jnp.where(here[2] < 2, send, jnp.zeros_like(send))


def enter_kernel(emb_scale, here, y_ref, *refs):
    found, out = refs[:-1], refs[-1]
    entering = (total_of(found) * emb_scale).astype(BF16)
    out[...] = jnp.where(here[2] == 0, entering, y_ref[...])


def head_kernel(n, flip, here, h_ref, gain_ref, table_ref, turned_ref, target_ref, *refs):
    normed_ref, raw_ref, scale_ref, out = refs
    size = out.shape[0] // n - EXTRA
    h = h_ref[...].astype(F32)
    scale = lax.rsqrt(jnp.mean(h * h, axis=0, keepdims=True) + EPS)
    normed = (h * scale * gain_ref[...].astype(F32)).astype(BF16)
    normed_ref[...] = normed
    raw = dot(table_ref[...], normed)
    raw_ref[...] = raw
    scale_ref[...] = rows_of(scale, 8)
    column = here[1] + lax.broadcasted_iota(jnp.int32, raw.shape, 0)
    target = jnp.where(here[2] % 2 == flip, target_ref[0:1, :], target_ref[1:2, :])
    hit = column == target
    capped = jnp.tanh(raw / LOGIT_CAP)
    others = jnp.where(hit, 0.0, jnp.exp(LOGIT_CAP * capped))
    weighted = others * (1.0 - capped * capped)
    extra = split_rows(
        [
            jnp.sum(others, axis=0, keepdims=True),
            jnp.sum(weighted * raw, axis=0, keepdims=True),
            jnp.sum(jnp.where(hit, raw, 0.0), axis=0, keepdims=True),
        ]
    )
    weighted = weighted.astype(BF16)
    for d in range(n):
        at = d * (size + EXTRA)
        term = dot(turned_ref[block_of(here, d, size), :], weighted)
        out[at : at + size, :] = term.astype(BF16)
        out[at + size : at + size + EXTRA, :] = extra


def add_terms(total, out):
    size = out.shape[0] - EXTRA
    out[:size, :] = total[:size, :].astype(BF16)
    out[size:, :] = split_rows(join_rows(total[size:, :], 3))


def pair_terms_kernel(here, keep_ref, got_ref, *outs):
    step = outs[0].shape[0]
    for d, out in enumerate(outs):
        cut = slice(d * step, (d + 1) * step)
        add_terms(keep_ref[cut, :].astype(F32) + got_ref[cut, :].astype(F32), out)


def sum_kernel(here, *refs):
    add_terms(total_of(refs[:-1]), refs[-1])


def cot_kernel(full, here, total_ref, scale_ref, h_ref, gain_ref, *refs):
    found, (out, sums_ref) = refs[:-2], refs[-2:]
    size, rows = h_ref.shape
    gain = gain_ref[block_of(here, 0, size), :].astype(F32)
    rest, weighted, raw_hit = join_rows(total_ref[size:, :].astype(F32), 3)
    capped = jnp.tanh(raw_hit / LOGIT_CAP)
    slope = 1.0 - capped * capped
    whole = rest + jnp.exp(LOGIT_CAP * capped)
    dhid = (total_ref[:size, :].astype(F32) - total_of(found) * (rest * slope)) / whole
    stat = (weighted - rest * slope * raw_hit) / whole
    scale = scale_ref[0:1, :]
    out[...] = (
        scale * gain * dhid - h_ref[...].astype(F32) * (scale * scale * stat / full)
    ).astype(BF16)
    place = lax.broadcasted_iota(jnp.int32, (8, rows), 0)
    sums = jnp.where(place == 0, rest, jnp.where(place == 1, raw_hit, 0.0))
    sums_ref[...] = jnp.where(here[2] == here[3] - 1, sums, 0.0)


def grad_kernel(ticks, emb_scale, here, ids_ref, targets_ref, sums_ref, *refs):
    out, loss_ref = refs[-2:]
    vocab, rows = refs[0].shape
    column = here[1] + lax.broadcasted_iota(jnp.int32, (vocab, rows), 0)
    place = lax.broadcasted_iota(jnp.int32, loss_ref.shape, 0)
    losses = jnp.zeros(loss_ref.shape, F32)
    for t in range(ticks):
        rest, raw_hit = sums_ref[8 * t : 8 * t + 1, :], sums_ref[8 * t + 1 : 8 * t + 2, :]
        logit = LOGIT_CAP * jnp.tanh(raw_hit / LOGIT_CAP)
        loss = jnp.mean(jnp.log(rest + jnp.exp(logit)) - logit, axis=1, keepdims=True)
        losses = jnp.where(place == t, jnp.broadcast_to(loss, losses.shape), losses)
    loss_ref[...] = losses
    dlogs, hits = [], []
    for flip in range(2):
        first = here[2] % 2 == flip
        sums = jnp.where(first, sums_ref[0:8, :], sums_ref[8:16, :])
        rest, raw_hit = sums[0:1, :], sums[1:2, :]
        whole = rest + jnp.exp(LOGIT_CAP * jnp.tanh(raw_hit / LOGIT_CAP))
        capped = jnp.tanh(refs[3 * flip][...] / LOGIT_CAP)
        hit = column == jnp.where(first, targets_ref[0:1, :], targets_ref[1:2, :])
        top = jnp.where(hit, -rest, jnp.exp(LOGIT_CAP * capped))
        dlogs.append((top / whole * (1.0 - capped * capped)).astype(BF16))
        hit = column == jnp.where(first, ids_ref[0:1, :], ids_ref[1:2, :])
        hits.append(hit.astype(F32).astype(BF16))
    full = out.shape[1]
    step = 256 if full % 256 == 0 else full
    for at in range(0, full, step):
        cut = slice(at, at + step)
        looked = sum(dot(hits[i], refs[3 * i + 2][cut, :], 1, 1) for i in range(2))
        heads = sum(dot(dlogs[i], refs[3 * i + 1][cut, :], 1, 1) for i in range(2))
        out[:, cut] = (heads + looked * emb_scale).astype(BF16)


def last_cots_kernel(here, gin_ref, cot_ref, out):
    out[...] = jnp.where(here[2] == here[3] - 1, cot_ref[...], gin_ref[...])


def after(x, *others):
    return lax.optimization_barrier((x, *others))[0]


def hop(x, pairs):
    return lax.ppermute(x, "section", pairs)


def swap(blocks):
    n = lax.axis_size("tensor")
    return [blocks[0]] + [
        lax.ppermute(blocks[d], "tensor", [(i, i ^ d) for i in range(n)]) for d in range(1, n)
    ]


def share(x):
    return swap([x] * lax.axis_size("tensor"))


def other_chips(root):
    core = root % 2
    return [
        2 * c + core for c in range(lax.axis_size("section") // 2) if c != root // 2
    ]


def from_chip(own, send, root):
    for s in other_chips(root):
        own = own + hop(send, [(root, s), (root ^ 1, s ^ 1)])
    return own


def to_chips(x, even_root, odd_root):
    sources = zip(other_chips(even_root), other_chips(odd_root))
    return [x] + [hop(x, [(a, even_root), (b, odd_root)]) for a, b in sources]


def other_core(x):
    return hop(x, [(i, i ^ 1) for i in range(lax.axis_size("section"))])


def body(
    fwd_in, back_in, stash, w_qkv, w_out, norm_gain, final_gain, table, ids, back_ids, targets
):
    pos = lax.axis_index("section")
    sections = lax.axis_size("section")
    tpos = lax.axis_index("tensor")
    n = lax.axis_size("tensor")
    rows, piece = fwd_in.shape[1:]
    full = piece * n
    vocab = table.shape[0]
    ticks = ids.shape[0]
    head = w_qkv.shape[-1]
    last = sections - 1
    emb_scale = math.sqrt(full)
    here = jnp.stack([tpos, (pos * n + tpos) * vocab, pos, jnp.full_like(pos, sections)])
    here = here.astype(jnp.int32)
    up = [(i, i + 1) for i in range(last)]
    down = [(i + 1, i) for i in range(last)]

    acts = fwd_in[0].T
    cots = back_in[0].T
    held0, held1 = stash[0, 0].T, stash[1, 0].T
    wq = w_qkv[0, :, :, 0, :].transpose(1, 0, 2)

    work = (2 * full * rows * 3 * head) + 4 * rows * rows * head
    act = ((piece, rows), BF16)
    wide = ((full, rows), BF16)
    message = ((piece + EXTRA, rows), BF16)
    whole_x = [pltpu.VMEM((full, rows), BF16)]

    *first, gain, fgain = call(
        functools.partial(prepare_kernel, n),
        [((2 * piece, rows), BF16)] * n + [wide] * 2,
        [here, acts, w_out[0, 0], norm_gain, final_gain[None]],
        "prepare",
        scratch=[pltpu.VMEM((full, head), BF16)],
    )
    base = swap(first)
    turned, *rows_found = call(
        lookup_kernel,
        [((full, vocab), BF16)] + [((full, ticks * rows), BF16)] * 2,
        [here, ids, targets, after(table, gain)],
        "lookup",
        4 * full * rows * vocab * ticks,
    )

    keep, send = rows_found
    found = call(
        functools.partial(pair_kernel, n), [act] * (n * ticks), [here, keep, other_core(send)], "pair"
    )

    def rows_of_tick(found, *others):
        found = after(swap(found), *others)
        return tree_sum([b.astype(F32) for b in found]).astype(BF16)

    def layer_out(x, got, earlier):
        return call(
            functools.partial(layer_out_kernel, n, piece),
            [act] * 3,
            [here, x, earlier, *got, *base],
            "layer_out",
            2 * piece * rows * head * n,
        )

    def back(got, saved):
        return call(
            functools.partial(back_kernel, n),
            [message] * n,
            [here, *got, *saved[:4], wq],
            "back",
            work,
        )

    def back_out(got, saved, x, last_x, cot, last_cot):
        return call(
            functools.partial(back_out_kernel, n, full),
            [act],
            [here, *got, saved[4], gain, x, last_x, cot, last_cot],
            "back_out",
        )

    def assemble(parts):
        return call(functools.partial(assemble_kernel, n), [wide], [here, *parts], "assemble")

    def run_head(h, flip):
        return call(
            functools.partial(head_kernel, n, flip),
            [wide, ((vocab, rows), F32), ((8, rows), F32), ((n * message[0][0], rows), BF16)],
            [here, h, fgain, table, turned, targets],
            "head",
            4 * full * rows * vocab,
        )

    def recompute(bs, tick):
        return call(
            functools.partial(recompute_kernel, n, tick),
            [
                ((3, head, rows), BF16),
                ((rows, head), BF16),
                ((rows, rows), F32),
                ((rows, rows), BF16),
                ((8, rows), F32),
            ],
            [here, *bs, *(base if tick > 0 else []), gain, wq],
            "recompute",
            work,
            whole_x,
        )

    messages = call(
        functools.partial(forward_parts_kernel, n, piece),
        [((2 * head, rows), BF16)] * n,
        [here, *base, gain, wq, cots],
        "forward",
        work,
        whole_x,
    )
    got0 = swap(messages)
    y0, _, _ = layer_out(acts, got0, acts)
    found0 = rows_of_tick(after(found[:n], y0))
    looked0 = to_chips(found0, 0, last)
    y0_even = hop(y0, [(last, last - 1)])
    saved0 = recompute(share(after(held0, found0)), 0)
    terms0 = back(got0, saved0)

    acts1 = call(
        functools.partial(enter_kernel, emb_scale),
        [act],
        [here, hop(y0, up), *looked0],
        "enter",
    )
    a1 = call(
        functools.partial(forward_kernel, n, piece),
        [((head, rows), BF16)],
        [here, *after(share(acts1), terms0[0]), gain, wq],
        "forward",
        work,
        whole_x,
    )
    y1, h_send, h_own = layer_out(acts1, share(a1), y0_even)

    gin0 = back_out(swap(after(terms0, y1)), saved0, held0, held0, cots, cots)
    saved1 = recompute(share(after(held1, a1)), 1)
    cots1 = hop(gin0, down)
    h_mine = after(from_chip(h_own, h_send, last), saved1[1])
    h_mine = assemble(after(share(h_mine), gin0))
    h_other = other_core(h_mine)

    normed_a, raw_a, scale_a, terms_a = run_head(h_mine, 0)
    normed_b, raw_b, scale_b, terms_b = run_head(h_other, 1)
    y1_up = hop(after(y1, h_mine), up)
    terms = call(
        pair_terms_kernel,
        [message] * n,
        [here, after(terms_a, y1_up, cots1), other_core(terms_b)],
        "pair_terms",
    )
    total = call(sum_kernel, [message], [here, *swap(terms)], "sum")
    found1 = rows_of_tick(after(found[n:], total))
    total = after(to_chips(total, last - 1, last), found1)
    total = call(sum_kernel, [message], [here, *total], "sum")
    looked1 = to_chips(after(found1, total), 0, last)

    def cot_of(total, scale, h, looked):
        return call(
            functools.partial(cot_kernel, full),
            [act, ((8, rows), F32)],
            [here, total, scale, h, fgain, *looked],
            "cot",
        )

    cot0, sums0 = cot_of(hop(total, [(last - 1, last)]), scale_b, y0, looked0)

    cot_parts = call(
        functools.partial(parts_kernel, n, piece),
        [((head, rows), BF16)] * n,
        [here, cots1, cot0, *base],
        "parts",
    )
    terms1 = back(after(swap(cot_parts), looked1), saved1)
    cot1, sums1 = cot_of(after(total, terms1[0]), scale_a, y1, looked1)
    sums = jnp.concatenate([sums0, sums1], axis=0)
    sums = sums + hop(sums, [(last, last - 1)])
    gin1 = back_out(after(swap(terms1), sums), saved1, held1, acts, cots1, cot0)
    g_send, g_own = call(pick_kernel, [act] * 2, [here, gin0, hop(gin1, [(0, 1)])], "pick")
    sums = from_chip(sums, sums, last)
    leaving_a = share(from_chip(g_own, g_send, 0))
    gin1_down = hop(gin1, down)
    acts2 = call(
        functools.partial(enter_kernel, emb_scale),
        [act],
        [here, y1_up, *after(looked1, gin1)],
        "enter",
    )
    leaving_a = assemble(after(leaving_a, acts2, sums, gin1_down))
    leaving_b = other_core(leaving_a)
    cots2 = call(last_cots_kernel, [act], [here, after(gin1_down, leaving_a), cot1], "last_cots")
    grad, losses = call(
        functools.partial(grad_kernel, ticks, emb_scale),
        [((vocab, full), BF16), ((8, rows), F32)],
        [
            *(here, back_ids, targets, sums),
            *(raw_a, normed_a, leaving_a),
            *(raw_b, normed_b, after(leaving_b, cots2)),
        ],
        "grad",
        8 * full * rows * vocab,
    )
    return (acts2.T[None], cots2.T[None], grad, losses[:ticks, 0])


def solution(mesh):
    return jax.shard_map(
        body,
        mesh=mesh,
        in_specs=(
            P("section", None, "tensor"),
            P("section", None, "tensor"),
            P(None, "section", None, "tensor"),
            P("section", None, None, "tensor", None),
            P("section", "tensor", None, None),
            P("section", None),
            P(),
            P(("section", "tensor"), None),
            P(),
            P(),
            P(),
        ),
        out_specs=(
            P("section", None, "tensor"),
            P("section", None, "tensor"),
            P(("section", "tensor"), None),
            P(),
        ),
        check_vma=False,
    )
```

```python
import functools
import math

import jax
import jax.numpy as jnp
from jax import lax
from jax.experimental import pallas as pl
from jax.experimental.pallas import tpu as pltpu
from jax.sharding import PartitionSpec as P

EPS = 1e-06
ATTN_CAP = 50.0
LOGIT_CAP = 30.0
F32 = jnp.float32
BF16 = jnp.bfloat16
EXTRA = 16


def dot(a, b, ca=1, cb=0):
    return lax.dot_general(a, b, (((ca,), (cb,)), ((), ())), preferred_element_type=F32)


def call(body, outs, args, name, flops=0, scratch=()):
    moved = sum(x.size * x.dtype.itemsize for x in args)
    moved += sum(math.prod(s) * jnp.dtype(d).itemsize for s, d in outs)
    vmem = pl.BlockSpec(memory_space=pltpu.VMEM)
    got = pl.pallas_call(
        body,
        out_shape=[jax.ShapeDtypeStruct(s, d) for s, d in outs],
        in_specs=[pl.BlockSpec(memory_space=pltpu.SMEM)] + [vmem] * (len(args) - 1),
        out_specs=[vmem] * len(outs),
        scratch_shapes=list(scratch),
        cost_estimate=pl.CostEstimate(flops=flops, bytes_accessed=moved, transcendentals=0),
        compiler_params=pltpu.CompilerParams(vmem_limit_bytes=24 << 20),
        name=name,
    )(*args)
    return got[0] if len(outs) == 1 else got


def block_of(here, d, size):
    return pl.ds(pl.multiple_of((here[0] ^ d) * size, size), size)


def rows_of(row, count):
    return jnp.broadcast_to(row, (count, row.shape[1]))


def split_rows(values):
    count = len(values)
    place = lax.broadcasted_iota(jnp.int32, (EXTRA, values[0].shape[1]), 0)
    out = jnp.zeros(place.shape, F32)
    for i, row in enumerate(values):
        high = row.astype(BF16).astype(F32)
        out = jnp.where(place == i, high, out)
        out = jnp.where(place == count + i, row - high, out)
    return out.astype(BF16)


def join_rows(extra, count):
    return [extra[i : i + 1, :] + extra[count + i : count + i + 1, :] for i in range(count)]


def tree_sum(parts):
    parts = list(parts)
    while len(parts) > 1:
        pairs = [parts[i] + parts[i + 1] for i in range(0, len(parts) - 1, 2)]
        parts = pairs + parts[len(parts) - len(parts) % 2 :]
    return parts[0]


def total_of(refs):
    return tree_sum([r[...].astype(F32) for r in refs])


def turn_column(row_ref, out_ref):
    full, width = out_ref.shape
    for at in range(0, full, width):
        part = jnp.broadcast_to(row_ref[0:1, at : at + width].astype(F32), (width, width))
        out_ref[at : at + width, :] = part.T.astype(BF16)


def prepare_kernel(n, here, x_ref, w_ref, gain_ref, fgain_ref, *refs):
    outs, (gcol_ref, fcol_ref, turned) = refs[:n], refs[n:]
    size = x_ref.shape[0]
    turned[...] = w_ref[...].T
    for d in range(n):
        outs[d][:size, :] = x_ref[...]
        outs[d][size:, :] = turned[block_of(here, d, size), :]
    turn_column(gain_ref, gcol_ref)
    turn_column(fgain_ref, fcol_ref)


def attend(x, gain, wq_ref):
    scale = lax.rsqrt(jnp.mean(x * x, axis=0, keepdims=True) + EPS)
    normed = (x * scale * gain).astype(BF16).T
    q = dot(normed, wq_ref[0]).astype(BF16)
    k = dot(normed, wq_ref[1]).astype(BF16)
    v = dot(normed, wq_ref[2]).astype(BF16)
    qt = q.T
    capped = jnp.tanh(dot(k, qt) * q.shape[1] ** -0.5 / ATTN_CAP)
    key = lax.broadcasted_iota(jnp.int32, capped.shape, 0)
    query = lax.broadcasted_iota(jnp.int32, capped.shape, 1)
    raised = jnp.where(key <= query, jnp.exp(ATTN_CAP * capped), 0.0)
    probs = (raised / jnp.sum(raised, axis=0, keepdims=True)).astype(BF16)
    return scale, qt, k, v, capped, probs


def forward_kernel(n, size, here, *refs):
    xs, (gain_ref, wq_ref, out, xfull) = refs[:n], refs[n:]
    for d in range(n):
        xfull[block_of(here, d, size), :] = xs[d][:size, :]
    x = xfull[...].astype(F32)
    _, _, _, v, _, probs = attend(x, gain_ref[...].astype(F32), wq_ref)
    out[...] = dot(v.T, probs).astype(BF16)


def forward_parts_kernel(n, size, here, *refs):
    xs, (gain_ref, wq_ref, cot_ref), outs, xfull = refs[:n], refs[n : n + 3], refs[n + 3 : -1], refs[-1]
    head = wq_ref.shape[-1]
    forward_kernel(n, size, here, *xs, gain_ref, wq_ref, outs[0].at[:head, :], xfull)
    for d in range(n):
        if d > 0:
            outs[d][:head, :] = outs[0][:head, :]
        part = dot(xs[d][size : 2 * size, :], cot_ref[...], 0, 0)
        outs[d][head:, :] = part.astype(BF16)


def recompute_kernel(n, tick, here, *refs):
    bs, refs = refs[:n], refs[n:]
    xs, refs = refs[: n * tick], refs[n * tick :]
    gain_ref, wq_ref, qkv_ref, v_ref, capped_ref, probs_ref, scale_ref, xfull = refs
    size = bs[0].shape[0]
    for d in range(n):
        block = bs[d][...]
        if tick > 0:
            block = jnp.where(here[2] == here[3] - 1, xs[d][:size, :], block)
        xfull[block_of(here, d, size), :] = block
    x = xfull[...].astype(F32)
    scale, qt, k, v, capped, probs = attend(x, gain_ref[...].astype(F32), wq_ref)
    qkv_ref[0] = qt
    qkv_ref[1] = k.T
    qkv_ref[2] = v.T
    v_ref[...] = v
    capped_ref[...] = capped
    probs_ref[...] = probs
    scale_ref[...] = rows_of(scale, 8)


def parts_kernel(n, size, here, cot_ref, last_cot_ref, *refs):
    wos, outs = refs[:n], refs[n:]
    cot = jnp.where(here[2] == here[3] - 1, last_cot_ref[...], cot_ref[...])
    for d in range(n):
        outs[d][...] = dot(wos[d][size : 2 * size, :], cot, 0, 0).astype(BF16)


def layer_out_kernel(n, size, here, x_ref, first_ref, *refs):
    got, wos, (out, send_ref, own_ref) = refs[:n], refs[n : 2 * n], refs[2 * n :]
    head = wos[0].shape[1]
    total = x_ref[...].astype(F32)
    for d in range(n):
        total = total + dot(wos[d][size : 2 * size, :], got[d][:head, :])
    y = total.astype(BF16)
    out[...] = y
    send = jnp.where(here[2] % 2 == 0, first_ref[...], y)
    send_ref[...] = send
    own_ref[...] = jnp.where(here[2] >= here[3] - 2, send, jnp.zeros_like(send))


def back_kernel(n, here, *refs):
    got, refs = refs[:n], refs[n:]
    qkv_ref, v_ref, capped_ref, probs_ref, wq_ref = refs[:5]
    outs = refs[5:]
    head = v_ref.shape[1]
    first = got[0].shape[0] - head
    da = sum(g[first:, :].astype(F32) for g in got).astype(BF16)
    probs = probs_ref[...]
    pfull = probs.astype(F32)
    dprob = dot(v_ref[...], da)
    dscore = pfull * (dprob - jnp.sum(dprob * pfull, axis=0, keepdims=True))
    capped = capped_ref[...]
    dlogit = (dscore * (1.0 - capped * capped) * head**-0.5).astype(BF16)
    grads = (
        dot(qkv_ref[1], dlogit).astype(BF16),
        dot(qkv_ref[0], dlogit, 1, 1).astype(BF16),
        dot(da, probs, 1, 1).astype(BF16),
    )
    stat = sum(
        jnp.sum(g.astype(F32) * qkv_ref[i].astype(F32), axis=0, keepdims=True)
        for i, g in enumerate(grads)
    )
    stat = split_rows([stat])
    size = outs[0].shape[0] - EXTRA
    for d in range(n):
        at = block_of(here, d, size)
        term = sum(dot(wq_ref[i, at, :], g) for i, g in enumerate(grads))
        outs[d][:size, :] = term.astype(BF16)
        outs[d][size:, :] = stat


def back_out_kernel(n, full, here, *refs):
    got, refs = refs[:n], refs[n:]
    scale_ref, gain_ref, x_ref, last_x_ref, cot_ref, last_cot_ref, out = refs
    size = x_ref.shape[0]
    total = total_of(got)
    (stat,) = join_rows(total[size:, :], 1)
    scale = scale_ref[0:1, :]
    gain = gain_ref[block_of(here, 0, size), :].astype(F32)
    is_last = here[2] == here[3] - 1
    x = jnp.where(is_last, last_x_ref[...], x_ref[...]).astype(F32)
    cot = jnp.where(is_last, last_cot_ref[...], cot_ref[...]).astype(F32)
    out[...] = (
        cot
        + scale * gain * total[:size, :]
        - x * (scale * scale * stat / full)
    ).astype(BF16)


def lookup_kernel(here, ids_ref, targets_ref, table_ref, turned_ref, *outs):
    turned_ref[...] = table_ref[...].T
    vocab = turned_ref.shape[1]
    ticks, rows = ids_ref.shape
    column = here[1] + lax.broadcasted_iota(jnp.int32, (vocab, rows), 0)
    even = here[2] % 2 == 0
    for t in range(ticks):
        ids, targets = ids_ref[t : t + 1, :], targets_ref[t : t + 1, :]
        wanted = (jnp.where(even, ids, targets), jnp.where(even, targets, ids))
        for out, row in zip(outs, wanted):
            hits = (column == row).astype(F32).astype(BF16)
            out[:, t * rows : (t + 1) * rows] = dot(turned_ref[...], hits).astype(BF16)


def pair_kernel(n, here, keep_ref, got_ref, *outs):
    size, rows = outs[0].shape
    for i, out in enumerate(outs):
        at, t = block_of(here, i % n, size), i // n
        cut = slice(t * rows, (t + 1) * rows)
        out[...] = (keep_ref[at, cut].astype(F32) + got_ref[at, cut].astype(F32)).astype(BF16)


def assemble_kernel(n, here, *refs):
    parts, out = refs[:n], refs[n]
    for d in range(n):
        out[block_of(here, d, parts[d].shape[0]), :] = parts[d][...]


def pick_kernel(here, even_ref, odd_ref, send_ref, own_ref):
    send = jnp.where(here[2] % 2 == 0, even_ref[...], odd_ref[...])
    send_ref[...] = send
    own_ref[...] = jnp.where(here[2] < 2, send, jnp.zeros_like(send))


def enter_kernel(emb_scale, here, y_ref, *refs):
    found, out = refs[:-1], refs[-1]
    entering = (total_of(found) * emb_scale).astype(BF16)
    out[...] = jnp.where(here[2] == 0, entering, y_ref[...])


def head_kernel(n, flip, here, h_ref, gain_ref, table_ref, turned_ref, target_ref, *refs):
    normed_ref, raw_ref, scale_ref, out = refs
    size = out.shape[0] // n - EXTRA
    h = h_ref[...].astype(F32)
    scale = lax.rsqrt(jnp.mean(h * h, axis=0, keepdims=True) + EPS)
    normed = (h * scale * gain_ref[...].astype(F32)).astype(BF16)
    normed_ref[...] = normed
    raw = dot(table_ref[...], normed)
    raw_ref[...] = raw
    scale_ref[...] = rows_of(scale, 8)
    column = here[1] + lax.broadcasted_iota(jnp.int32, raw.shape, 0)
    target = jnp.where(here[2] % 2 == flip, target_ref[0:1, :], target_ref[1:2, :])
    hit = column == target
    capped = jnp.tanh(raw / LOGIT_CAP)
    others = jnp.where(hit, 0.0, jnp.exp(LOGIT_CAP * capped))
    weighted = others * (1.0 - capped * capped)
    extra = split_rows(
        [
            jnp.sum(others, axis=0, keepdims=True),
            jnp.sum(weighted * raw, axis=0, keepdims=True),
            jnp.sum(jnp.where(hit, raw, 0.0), axis=0, keepdims=True),
        ]
    )
    weighted = weighted.astype(BF16)
    for d in range(n):
        at = d * (size + EXTRA)
        term = dot(turned_ref[block_of(here, d, size), :], weighted)
        out[at : at + size, :] = term.astype(BF16)
        out[at + size : at + size + EXTRA, :] = extra


def add_terms(total, out):
    size = out.shape[0] - EXTRA
    out[:size, :] = total[:size, :].astype(BF16)
    out[size:, :] = split_rows(join_rows(total[size:, :], 3))


def pair_terms_kernel(here, keep_ref, got_ref, *outs):
    step = outs[0].shape[0]
    for d, out in enumerate(outs):
        cut = slice(d * step, (d + 1) * step)
        add_terms(keep_ref[cut, :].astype(F32) + got_ref[cut, :].astype(F32), out)


def sum_kernel(here, *refs):
    add_terms(total_of(refs[:-1]), refs[-1])


def sum_chips_kernel(here, *refs):
    parts, (out, sums_ref) = refs[:-2], refs[-2:]
    total = total_of(parts)
    add_terms(total, out)
    rest, _, raw_hit = join_rows(total[out.shape[0] - EXTRA :, :], 3)
    place = lax.broadcasted_iota(jnp.int32, sums_ref.shape, 0)
    sums = jnp.where(place == 0, rest, jnp.where(place == 1, raw_hit, 0.0))
    sums_ref[...] = jnp.where(here[2] >= here[3] - 2, sums, 0.0)


def cot_kernel(full, here, total_ref, scale_ref, h_ref, gain_ref, *refs):
    found, out = refs[:-1], refs[-1]
    size = h_ref.shape[0]
    gain = gain_ref[block_of(here, 0, size), :].astype(F32)
    rest, weighted, raw_hit = join_rows(total_ref[size:, :].astype(F32), 3)
    capped = jnp.tanh(raw_hit / LOGIT_CAP)
    slope = 1.0 - capped * capped
    whole = rest + jnp.exp(LOGIT_CAP * capped)
    dhid = (total_ref[:size, :].astype(F32) - total_of(found) * (rest * slope)) / whole
    stat = (weighted - rest * slope * raw_hit) / whole
    scale = scale_ref[0:1, :]
    out[...] = (
        scale * gain * dhid - h_ref[...].astype(F32) * (scale * scale * stat / full)
    ).astype(BF16)


def grad_kernel(ticks, emb_scale, here, ids_ref, targets_ref, *refs):
    out, loss_ref = refs[-2:]
    vocab, rows = refs[1].shape
    column = here[1] + lax.broadcasted_iota(jnp.int32, (vocab, rows), 0)
    place = lax.broadcasted_iota(jnp.int32, loss_ref.shape, 0)
    losses = jnp.zeros(loss_ref.shape, F32)
    dlogs, hits = [], []
    for flip in range(2):
        first = here[2] % 2 == flip
        rest, raw_hit = refs[4 * flip][0:1, :], refs[4 * flip][1:2, :]
        logit = LOGIT_CAP * jnp.tanh(raw_hit / LOGIT_CAP)
        whole = rest + jnp.exp(logit)
        loss = jnp.mean(jnp.log(whole) - logit, axis=1, keepdims=True)
        tick = jnp.where(first, 0, 1)
        losses = jnp.where(place == tick, jnp.broadcast_to(loss, losses.shape), losses)
        capped = jnp.tanh(refs[4 * flip + 1][...] / LOGIT_CAP)
        hit = column == jnp.where(first, targets_ref[0:1, :], targets_ref[1:2, :])
        top = jnp.where(hit, -rest, jnp.exp(LOGIT_CAP * capped))
        dlogs.append((top / whole * (1.0 - capped * capped)).astype(BF16))
        hit = column == jnp.where(first, ids_ref[0:1, :], ids_ref[1:2, :])
        hits.append(hit.astype(F32).astype(BF16))
    loss_ref[...] = losses
    full = out.shape[1]
    step = 256 if full % 256 == 0 else full
    for at in range(0, full, step):
        cut = slice(at, at + step)
        looked = sum(dot(hits[i], refs[4 * i + 3][cut, :], 1, 1) for i in range(2))
        heads = sum(dot(dlogs[i], refs[4 * i + 2][cut, :], 1, 1) for i in range(2))
        out[:, cut] = (heads + looked * emb_scale).astype(BF16)


def last_cots_kernel(here, gin_ref, cot_ref, out):
    out[...] = jnp.where(here[2] == here[3] - 1, cot_ref[...], gin_ref[...])


def after(x, *others):
    return lax.optimization_barrier((x, *others))[0]


def hop(x, pairs):
    return lax.ppermute(x, "section", pairs)


def swap(blocks):
    n = lax.axis_size("tensor")
    return [blocks[0]] + [
        lax.ppermute(blocks[d], "tensor", [(i, i ^ d) for i in range(n)]) for d in range(1, n)
    ]


def share(x):
    return swap([x] * lax.axis_size("tensor"))


def other_chips(root):
    core = root % 2
    return [
        2 * c + core for c in range(lax.axis_size("section") // 2) if c != root // 2
    ]


def from_chip(own, send, root):
    for s in other_chips(root):
        own = own + hop(send, [(root, s), (root ^ 1, s ^ 1)])
    return own


def to_chips(x, even_root, odd_root):
    sources = zip(other_chips(even_root), other_chips(odd_root))
    return [x] + [hop(x, [(a, even_root), (b, odd_root)]) for a, b in sources]


def other_core(x):
    return hop(x, [(i, i ^ 1) for i in range(lax.axis_size("section"))])


def body(
    fwd_in, back_in, stash, w_qkv, w_out, norm_gain, final_gain, table, ids, back_ids, targets
):
    pos = lax.axis_index("section")
    sections = lax.axis_size("section")
    tpos = lax.axis_index("tensor")
    n = lax.axis_size("tensor")
    rows, piece = fwd_in.shape[1:]
    full = piece * n
    vocab = table.shape[0]
    ticks = ids.shape[0]
    head = w_qkv.shape[-1]
    last = sections - 1
    emb_scale = math.sqrt(full)
    here = jnp.stack([tpos, (pos * n + tpos) * vocab, pos, jnp.full_like(pos, sections)])
    here = here.astype(jnp.int32)
    up = [(i, i + 1) for i in range(last)]
    down = [(i + 1, i) for i in range(last)]

    acts = fwd_in[0].T
    cots = back_in[0].T
    held0, held1 = stash[0, 0].T, stash[1, 0].T
    wq = w_qkv[0, :, :, 0, :].transpose(1, 0, 2)

    work = (2 * full * rows * 3 * head) + 4 * rows * rows * head
    act = ((piece, rows), BF16)
    wide = ((full, rows), BF16)
    message = ((piece + EXTRA, rows), BF16)
    whole_x = [pltpu.VMEM((full, rows), BF16)]

    *first, gain, fgain = call(
        functools.partial(prepare_kernel, n),
        [((2 * piece, rows), BF16)] * n + [wide] * 2,
        [here, acts, w_out[0, 0], norm_gain, final_gain[None]],
        "prepare",
        scratch=[pltpu.VMEM((full, head), BF16)],
    )
    base = swap(first)
    turned, *rows_found = call(
        lookup_kernel,
        [((full, vocab), BF16)] + [((full, ticks * rows), BF16)] * 2,
        [here, ids, targets, after(table, gain)],
        "lookup",
        4 * full * rows * vocab * ticks,
    )

    keep, send = rows_found
    found = call(
        functools.partial(pair_kernel, n), [act] * (n * ticks), [here, keep, other_core(send)], "pair"
    )

    def rows_of_tick(found, *others):
        found = after(swap(found), *others)
        return tree_sum([b.astype(F32) for b in found]).astype(BF16)

    def layer_out(x, got, earlier):
        return call(
            functools.partial(layer_out_kernel, n, piece),
            [act] * 3,
            [here, x, earlier, *got, *base],
            "layer_out",
            2 * piece * rows * head * n,
        )

    def back(got, saved):
        return call(
            functools.partial(back_kernel, n),
            [message] * n,
            [here, *got, *saved[:4], wq],
            "back",
            work,
        )

    def back_out(got, saved, x, last_x, cot, last_cot):
        return call(
            functools.partial(back_out_kernel, n, full),
            [act],
            [here, *got, saved[4], gain, x, last_x, cot, last_cot],
            "back_out",
        )

    def assemble(parts):
        return call(functools.partial(assemble_kernel, n), [wide], [here, *parts], "assemble")

    def run_head(h, flip):
        return call(
            functools.partial(head_kernel, n, flip),
            [wide, ((vocab, rows), F32), ((8, rows), F32), ((n * message[0][0], rows), BF16)],
            [here, h, fgain, table, turned, targets],
            "head",
            4 * full * rows * vocab,
        )

    def recompute(bs, tick):
        return call(
            functools.partial(recompute_kernel, n, tick),
            [
                ((3, head, rows), BF16),
                ((rows, head), BF16),
                ((rows, rows), F32),
                ((rows, rows), BF16),
                ((8, rows), F32),
            ],
            [here, *bs, *(base if tick > 0 else []), gain, wq],
            "recompute",
            work,
            whole_x,
        )

    messages = call(
        functools.partial(forward_parts_kernel, n, piece),
        [((2 * head, rows), BF16)] * n,
        [here, *base, gain, wq, cots],
        "forward",
        work,
        whole_x,
    )
    got0 = swap(messages)
    y0, _, _ = layer_out(acts, got0, acts)
    found0 = rows_of_tick(after(found[:n], y0))
    looked0 = to_chips(found0, 0, last)
    y0_even = hop(y0, [(last, last - 1)])
    saved0 = recompute(share(after(held0, found0)), 0)
    terms0 = back(got0, saved0)

    acts1 = call(
        functools.partial(enter_kernel, emb_scale),
        [act],
        [here, hop(y0, up), *looked0],
        "enter",
    )
    a1 = call(
        functools.partial(forward_kernel, n, piece),
        [((head, rows), BF16)],
        [here, *after(share(acts1), terms0[0]), gain, wq],
        "forward",
        work,
        whole_x,
    )
    y1, h_send, h_own = layer_out(acts1, share(a1), y0_even)

    gin0 = back_out(swap(after(terms0, y1)), saved0, held0, held0, cots, cots)
    saved1 = recompute(share(after(held1, a1)), 1)
    cots1 = hop(gin0, down)
    h_mine = after(from_chip(h_own, h_send, last), saved1[1])
    h_mine = assemble(after(share(h_mine), gin0))
    h_other = other_core(h_mine)

    normed_a, raw_a, scale_a, terms_a = run_head(h_mine, 0)
    normed_b, raw_b, scale_b, terms_b = run_head(h_other, 1)
    y1_up = hop(after(y1, h_mine), up)
    terms = call(
        pair_terms_kernel,
        [message] * n,
        [here, after(terms_a, y1_up, cots1), other_core(terms_b)],
        "pair_terms",
    )
    total = call(sum_kernel, [message], [here, *swap(terms)], "sum")
    found1 = rows_of_tick(after(found[n:], total))
    total = after(to_chips(total, last - 1, last), found1)
    total, sums = call(
        sum_chips_kernel, [message, ((8, rows), F32)], [here, *total], "sum_chips"
    )
    looked1 = to_chips(after(found1, total), 0, last)

    def cot_of(total, scale, h, looked):
        return call(
            functools.partial(cot_kernel, full),
            [act],
            [here, total, scale, h, fgain, *looked],
            "cot",
        )

    cot0 = cot_of(hop(total, [(last - 1, last)]), scale_b, y0, looked0)

    cot_parts = call(
        functools.partial(parts_kernel, n, piece),
        [((head, rows), BF16)] * n,
        [here, cots1, cot0, *base],
        "parts",
    )
    terms1 = back(after(swap(cot_parts), looked1), saved1)
    cot1 = cot_of(after(total, terms1[0]), scale_a, y1, looked1)
    sums = after(sums, cot_parts)
    sums_a = from_chip(sums, sums, last)
    gin1 = back_out(after(swap(terms1), cot1, sums_a), saved1, held1, acts, cots1, cot0)
    g_send, g_own = call(pick_kernel, [act] * 2, [here, gin0, hop(gin1, [(0, 1)])], "pick")
    sums_b = other_core(after(sums_a, g_send))
    leaving_a = share(from_chip(g_own, g_send, 0))
    gin1_down = hop(gin1, down)
    acts2 = call(
        functools.partial(enter_kernel, emb_scale),
        [act],
        [here, y1_up, *after(looked1, gin1)],
        "enter",
    )
    leaving_a = assemble(after(leaving_a, acts2, sums_b, gin1_down))
    leaving_b = other_core(leaving_a)
    cots2 = call(last_cots_kernel, [act], [here, after(gin1_down, leaving_a), cot1], "last_cots")
    grad, losses = call(
        functools.partial(grad_kernel, ticks, emb_scale),
        [((vocab, full), BF16), ((8, rows), F32)],
        [
            *(here, back_ids, targets),
            *(sums_a, raw_a, normed_a, leaving_a),
            *(sums_b, raw_b, normed_b, after(leaving_b, cots2)),
        ],
        "grad",
        8 * full * rows * vocab,
    )
    return (acts2.T[None], cots2.T[None], grad, losses[:ticks, 0])


def solution(mesh):
    return jax.shard_map(
        body,
        mesh=mesh,
        in_specs=(
            P("section", None, "tensor"),
            P("section", None, "tensor"),
            P(None, "section", None, "tensor"),
            P("section", None, None, "tensor", None),
            P("section", "tensor", None, None),
            P("section", None),
            P(),
            P(("section", "tensor"), None),
            P(),
            P(),
            P(),
        ),
        out_specs=(
            P("section", None, "tensor"),
            P("section", None, "tensor"),
            P(("section", "tensor"), None),
            P(),
        ),
        check_vma=False,
    )
```
